256 devices in a mesh: depth: 32 (over z, x), replica: 8 (over y, core).
Axes of the slice: x: 4, y: 4, z: 8, core: 2. Of those that a mesh axis runs over, the one named last changes fastest.
Arguments:
- volume: bfloat16 [8, 64, 16, 16, 256], P('replica', 'depth'), may hold values from -8 to 8, as said below
- cotangent: bfloat16 [8, 64, 16, 16, 256], P('replica', 'depth'), may hold values from -8 to 8, as said below
- kernel: bfloat16 [3, 3, 3, 256, 256], replicated, may hold values from -0.078125 to 0.078125
Outputs:
- grad_volume: bfloat16 [8, 64, 16, 16, 256], P('replica', 'depth')
- merged_grad: float32 [6912, 256], P('depth', 'replica')
The draws below stay inside these ranges and needn't reach their ends.
Inputs may be any that keep to these rules, and one draw needn't show every extreme that they name: `volume`: input fields, independent across voxels and channels. cotangent entries, independent across voxels and channels.
All inputs are finite; a program needn't handle non-finite values.
Results may differ from the reference program's by a relative error of at most 0.0019.
The reference program's roundings to bfloat16 on the way (of `pre_grad`) count: a program that leaves them out, or rounds other values in their place, can miss the bound.
Values may be sent and summed in bfloat16 or wider, within the bound.
A program may use at most 128 MiB of HBM per device.

```python
import math
import jax
import jax.numpy as jnp
import numpy as np
from jax import lax

C = 256
H = 16
W = 16
NZ = 64
VOLUMES = 8


def draw_volume(key, part):
    shared = jax.random.normal(jax.random.fold_in(key, 11), (1, NZ, H, W, C), jnp.float32)
    owned = jax.random.normal(jax.random.fold_in(key, 12), (VOLUMES, NZ, H, W, C), jnp.float32)
    placed = jnp.arange(NZ, dtype=jnp.float32) / (NZ - 1)
    depth_ramp = 0.6 + 1.2 * placed
    values = (0.6 * shared + 0.8 * owned) * depth_ramp[None, :, None, None, None]
    return jnp.clip(values, -8.0, 8.0).astype(jnp.bfloat16)


def draw_cotangent(key, part):
    shared = jax.random.normal(jax.random.fold_in(key, 21), (1, NZ, H, W, C), jnp.float32)
    owned = jax.random.normal(jax.random.fold_in(key, 22), (VOLUMES, NZ, H, W, C), jnp.float32)
    ranks = jax.random.permutation(jax.random.fold_in(key, 26), VOLUMES).astype(jnp.float32)
    amplitude = jnp.exp2(-1.0 + 1.7 * ranks / (VOLUMES - 1))
    mixing = jax.random.uniform(jax.random.fold_in(key, 27), (VOLUMES,), jnp.float32, 0.25, 0.85)
    remainder = jnp.sqrt(1.0 - mixing * mixing)
    amplitude = amplitude[:, None, None, None, None]
    mixing = mixing[:, None, None, None, None]
    remainder = remainder[:, None, None, None, None]
    values = (mixing * shared + remainder * owned) * amplitude
    return jnp.clip(values, -8.0, 8.0).astype(jnp.bfloat16)


def gaussian(stream_key, shape, deviation, most, held_as=jnp.bfloat16):
    drawn = jax.random.normal(stream_key, shape, jnp.float32) * deviation
    return jnp.minimum(jnp.maximum(drawn, -most), most).astype(held_as)


def setup_inputs(seed: int = 0) -> dict:
    key_of = jax.random.split(jax.random.key(seed), 4)
    return {
        "volume": draw_volume(jax.random.fold_in(key_of[3], 71), 0),
        "cotangent": draw_cotangent(jax.random.fold_in(key_of[3], 71), 0),
        "kernel": gaussian(key_of[2], (3, 3, 3, C, C), (27 * C) ** -0.5, 0.078125),
    }


epsilon = 1e-06

def conv_same(field, weights):
    return lax.conv_general_dilated(field[None], weights, (1, 1, 1), 'SAME', dimension_numbers=('NDHWC', 'DHWIO', 'NDHWC'), precision=lax.Precision.HIGHEST)[0]

def reference(volume, cotangent, kernel):
    factor = 1.0 / math.sqrt(NZ * H * W)
    kernel32 = kernel.astype(jnp.float32)
    kernel_flip = kernel32[::-1, ::-1, ::-1].transpose(0, 1, 2, 4, 3)
    grad_fields = []
    replica_grads = []
    for member in range(VOLUMES):
        volume32 = volume[member].astype(jnp.float32)
        preact = conv_same(volume32, kernel32)
        sigmoid_val = jax.nn.sigmoid(preact)
        pre_grad = (cotangent[member].astype(jnp.float32) * sigmoid_val * (1.0 + preact * (1.0 - sigmoid_val))).astype(jnp.bfloat16)
        pre_grad32 = pre_grad.astype(jnp.float32)
        grad_fields.append(conv_same(pre_grad32, kernel_flip).astype(jnp.bfloat16))
        padded = jnp.pad(volume32, ((1, 1), (1, 1), (1, 1), (0, 0)))
        flat_grad = pre_grad32.reshape(-1, C)
        blocks = []
        for depth_off in range(3):
            for row_off in range(3):
                for col_off in range(3):
                    window = padded[depth_off:depth_off + NZ, row_off:row_off + H, col_off:col_off + W, :].reshape(-1, C)
                    blocks.append(jnp.dot(window.T, flat_grad, precision=lax.Precision.HIGHEST))
        replica_grads.append(jnp.concatenate(blocks, 0) * factor)
    stacked = jnp.stack(replica_grads)
    replica_ids = np.arange(VOLUMES)
    stride = 1
    while stride < VOLUMES:
        partner = stacked[replica_ids ^ stride]
        inner_prod = lax.optimization_barrier(jnp.sum(stacked * partner, axis=(1, 2)))[:, None, None]
        own_norm = lax.optimization_barrier(jnp.sum(stacked * stacked, axis=(1, 2)))[:, None, None]
        partner_norm = lax.optimization_barrier(jnp.sum(partner * partner, axis=(1, 2)))[:, None, None]
        stacked = (1.0 - inner_prod / (2.0 * (own_norm + epsilon))) * stacked + (1.0 - inner_prod / (2.0 * (partner_norm + epsilon))) * partner
        stride = stride * 2
    return (jnp.stack(grad_fields), stacked[0])
```

```python
import functools

import jax
import jax.numpy as jnp
from jax import lax
from jax.experimental import pallas as pl
from jax.experimental.pallas import tpu as pltpu
from jax.sharding import PartitionSpec as P

MESH = pl.DeviceIdType.MESH
EPS = 1e-06
F32, BF16 = jnp.float32, jnp.bfloat16
NX, NZ, NR = 4, 8, 8
FACTOR = 1.0 / 128.0

RIGHT = ((4, 0), (3, 1), (3, 0), (2, 1), (2, 0), (1, 1), (1, 0))
LEFT = ((4, 1), (3, 0), (3, 1), (2, 0), (2, 1), (1, 0), (1, 1))


def rcopy(src, dst, ss, rs, dev):
    return pltpu.make_async_remote_copy(
        src_ref=src, dst_ref=dst, send_sem=ss, recv_sem=rs, device_id=dev, device_id_type=MESH
    )


def adasum_weights(gram):
    groups = [[(v, None)] for v in range(NR)]
    dots = dict(gram)
    count = NR
    weights = [None] * NR
    members = [[v] for v in range(NR)]
    while count > 1:
        alpha = [None] * count
        for a in range(0, count, 2):
            b = a + 1
            half = 0.5 * dots[(a, b)]
            alpha[a] = 1.0 - half / (jnp.maximum(dots[(a, a)], 0.0) + EPS)
            alpha[b] = 1.0 - half / (jnp.maximum(dots[(b, b)], 0.0) + EPS)
        for a in range(count):
            for v in members[a]:
                weights[v] = alpha[a] if weights[v] is None else weights[v] * alpha[a]
        merged = {}
        half_count = count // 2
        for i in range(half_count):
            for j in range(i, half_count):
                total = None
                for a in (2 * i, 2 * i + 1):
                    for b in (2 * j, 2 * j + 1):
                        term = alpha[a] * alpha[b] * dots[(min(a, b), max(a, b))]
                        total = term if total is None else total + term
                merged[(i, j)] = total
        members = [members[2 * i] + members[2 * i + 1] for i in range(half_count)]
        dots = merged
        count = half_count
    return weights


def kernel(
    vol, cot, kern,
    gout, mout,
    x10, wk, cotv, ybuf, gbuf, gts, gtall, g3, acc, rsb, rfin, fsend, frecv, gr1, gr2, gr3, gsrc,
    lsem, xss, xrs, gss, grs, hss, hrs, rss, rrs, fss, frs, a1s, a1r, a2s, a2r, a3s, a3r,
):
    d = lax.axis_index("depth")
    rep = lax.axis_index("replica")
    z = d // NX
    x = lax.rem(d, NX)
    xr, xl = lax.rem(x + 1, NX), lax.rem(x + 3, NX)
    xo = lax.rem(x + 2, NX)
    zr, zl = lax.rem(z + 1, NZ), lax.rem(z + 7, NZ)

    bar = pltpu.get_barrier_semaphore()

    def greet(dd, rr):
        pl.semaphore_signal(bar, inc=1, device_id=(dd, rr), device_id_type=MESH)

    for dx in range(NX):
        for dr in range(NR):
            if dx or dr:
                greet(z * NX + lax.rem(x + dx, NX), lax.rem(rep + dr, NR))
    for dz in range(1, NZ):
        greet(lax.rem(z + dz, NZ) * NX + x, rep)

    @pl.when((x == 3) & (z < NZ - 1))
    def _():
        greet(d + 1, rep)

    @pl.when((x == 0) & (z > 0))
    def _():
        greet(d - 1, rep)

    rows = pl.ds(16, 256)
    lx = [pltpu.make_async_copy(vol.at[p], x10.at[1 + 2 * x + p, rows], lsem.at[p]) for p in range(2)]
    lw = pltpu.make_async_copy(kern, wk, lsem.at[2])
    lc = pltpu.make_async_copy(cot, cotv, lsem.at[3])
    for c in lx:
        c.start()
    lw.start()
    lc.start()
    pad = jnp.zeros((16, 256), BF16)
    for k in range(10):
        x10[k, 0:16, :] = pad
        x10[k, 272:288, :] = pad
    for k in range(4):
        gbuf[k, 0:16, :] = pad
        gbuf[k, 272:288, :] = pad

    @pl.when(z == 0)
    def _():
        x10[0, 16:272, :] = jnp.zeros((256, 256), BF16)

    @pl.when(z == NZ - 1)
    def _():
        x10[9, 16:272, :] = jnp.zeros((256, 256), BF16)

    @pl.when(d == 0)
    def _():
        gbuf[0, 16:272, :] = jnp.zeros((256, 256), BF16)

    @pl.when(d == NX * NZ - 1)
    def _():
        gbuf[3, 16:272, :] = jnp.zeros((256, 256), BF16)

    across = ((x == 3) & (z < NZ - 1)) | ((x == 0) & (z > 0))
    pl.semaphore_wait(bar, NX * NR - 1 + NZ - 1 + across.astype(jnp.int32))

    dr_, dl_ = z * NX + xr, z * NX + xl

    def plane(owner, p):
        return x10.at[1 + 2 * owner + p, rows]

    def to_right(p):
        return rcopy(vol.at[p], plane(x, p), xss.at[p], xrs.at[p], (dr_, rep))

    def to_left(p):
        return rcopy(vol.at[p], plane(x, p), xss.at[2 + p], xrs.at[2 + p], (dl_, rep))

    def from_left(p):
        return rcopy(vol.at[p], plane(xl, p), xss.at[p], xrs.at[p], (dr_, rep))

    def from_right(p):
        return rcopy(vol.at[p], plane(xr, p), xss.at[2 + p], xrs.at[2 + p], (dl_, rep))

    relay_r = rcopy(plane(xl, 0), plane(xl, 0), xss.at[4], xrs.at[4], (dr_, rep))
    relay_l = rcopy(plane(xr, 1), plane(xr, 1), xss.at[5], xrs.at[5], (dl_, rep))
    from_relay_l = rcopy(plane(xo, 0), plane(xo, 0), xss.at[4], xrs.at[4], (dr_, rep))
    from_relay_r = rcopy(plane(xo, 1), plane(xo, 1), xss.at[5], xrs.at[5], (dl_, rep))

    low, high = x10.at[0, rows], x10.at[9, rows]
    up_first = rcopy(vol.at[1], low, xss.at[6], xrs.at[6], (lax.rem(d + 1, NX * NZ), rep))
    down_first = rcopy(vol.at[0], high, xss.at[7], xrs.at[7], (lax.rem(d + NX * NZ - 1, NX * NZ), rep))
    up_last = rcopy(x10.at[8, rows], low, xss.at[8], xrs.at[6], (zr * NX + x, rep))
    down_last = rcopy(x10.at[1, rows], high, xss.at[9], xrs.at[7], (zl * NX + x, rep))

    @pl.when((x == 3) & (z < NZ - 1))
    def _():
        up_first.start()

    @pl.when((x == 0) & (z > 0))
    def _():
        down_first.start()

    to_right(1).start()
    to_left(0).start()
    to_right(0).start()
    to_left(1).start()

    for c in lx:
        c.wait()
    lw.wait()
    for p in range(2):
        taps = [(kd, kh) for kd in ((1, 2) if p == 0 else (0, 1)) for kh in range(3)]
        lhs = jnp.concatenate(
            [x10[2 * x + p + kd, kh * 16 : kh * 16 + 256, :] for kd, kh in taps], axis=1
        )
        for kw in range(3):
            rhs = jnp.concatenate([wk[kd * 3 + kh, kw] for kd, kh in taps], axis=0)
            ybuf[p, kw] = jnp.dot(lhs, rhs, preferred_element_type=F32)
    lc.wait()

    from_left(1).wait_recv()
    from_right(0).wait_recv()

    @pl.when((x == 0) & (z > 0))
    def _():
        up_first.wait_recv()

    @pl.when((x == 3) & (z < NZ - 1))
    def _():
        down_first.wait_recv()

    relay_l_ready = None
    w_of = lax.rem(lax.broadcasted_iota(jnp.int32, (256, 256), 0), 16)
    for p in range(2):
        kd = 0 if p == 0 else 2
        lhs = jnp.concatenate(
            [x10[2 * x + p + kd, kh * 16 : kh * 16 + 256, :] for kh in range(3)], axis=1
        )
        y = []
        for kw in range(3):
            rhs = jnp.concatenate([wk[kd * 3 + kh, kw] for kh in range(3)], axis=0)
            y.append(ybuf[p, kw] + jnp.dot(lhs, rhs, preferred_element_type=F32))
        preact = (
            y[1]
            + jnp.where(w_of >= 1, pltpu.roll(y[0], 1, 0), 0.0)
            + jnp.where(w_of <= 14, pltpu.roll(y[2], 255, 0), 0.0)
        )
        s = jax.nn.sigmoid(preact)
        g = (cotv[p].astype(F32) * s * (1.0 + preact * (1.0 - s))).astype(BF16)
        gbuf[1 + p, 16:272, :] = g
        gt = g.astype(F32).T.astype(BF16)
        for q in range(NX):
            gts[q, :, p * 256 : p * 256 + 256] = gt[q * 64 : q * 64 + 64, :]

    def g_send(dx):
        q = lax.rem(x + dx, NX)
        return rcopy(gts.at[q], gtall.at[x], gss.at[dx], grs.at[dx], (z * NX + q, rep))

    def g_recv(dx):
        q = lax.rem(x + NX - dx, NX)
        return rcopy(gts.at[q], gtall.at[q], gss.at[dx], grs.at[dx], (z * NX + q, rep))

    for dx in (2, 1, 3):
        g_send(dx).start()
    gtall[x] = gts[x]

    from_left(0).wait_recv()
    relay_r.start()
    from_right(1).wait_recv()
    relay_l.start()

    from_relay_l.wait_recv()
    from_relay_r.wait_recv()

    @pl.when((z < NZ - 1) & (x != 0))
    def _():
        up_last.start()

    @pl.when((z > 0) & (x != 3))
    def _():
        down_last.start()

    g_up = rcopy(gbuf.at[2, rows], gbuf.at[0, rows], hss.at[0], hrs.at[0], (lax.rem(d + 1, NX * NZ), rep))
    g_down = rcopy(
        gbuf.at[1, rows], gbuf.at[3, rows], hss.at[1], hrs.at[1], (lax.rem(d + NX * NZ - 1, NX * NZ), rep)
    )

    @pl.when(d < NX * NZ - 1)
    def _():
        g_up.start()

    @pl.when(d > 0)
    def _():
        g_down.start()

    for dx in (1, 3, 2):
        g_recv(dx).wait_recv()
    lane = lax.rem(lax.broadcasted_iota(jnp.int32, (64, 512), 1), 16)
    for q in range(NX):
        t = gtall[q].astype(F32)
        cols = slice(q * 512, q * 512 + 512)
        g3[0:64, cols] = jnp.where(lane <= 14, pltpu.roll(t, 511, 1), 0.0).astype(BF16)
        g3[64:128, cols] = t.astype(BF16)
        last = jnp.where(lane >= 1, pltpu.roll(t, 1, 1), 0.0).astype(BF16)
        g3[128:192, cols] = last
        g3[192:256, cols] = last

    @pl.when((z > 0) & (x != 0))
    def _():
        up_last.wait_recv()

    @pl.when((z < NZ - 1) & (x != 3))
    def _():
        down_last.wait_recv()

    for b in range(9):
        kd, kh = b // 3, b % 3
        field = x10[kd : kd + 8, kh * 16 : kh * 16 + 256, :].reshape(2048, 256)
        out = jnp.dot(g3[...], field, preferred_element_type=F32).T
        pair, twice = out[:, 0:128], out[:, 128:256]
        swapped = pltpu.roll(pair, 64, 1)
        for kw in range(3):
            start = (3 * b + kw) * 256
            at = start
            while at < start + 256:
                block = at // 216
                end = min(start + 256, (block + 1) * 216)
                k, q = block // 4, block % 4
                side, h = q // 2, q % 2
                source = twice if kw == 2 else (pair if kw == side else swapped)
                acc[k, h, at - block * 216 : end - block * 216, side * 64 : side * 64 + 64] = source[
                    at - start : end - start, side * 64 : side * 64 + 64
                ]
                at = end

    def unit(side, j):
        dist, h = (RIGHT, LEFT)[side][j]
        k = lax.rem(z + dist, NZ) if side == 0 else lax.rem(z + NZ - dist, NZ)
        there = zr if side == 0 else zl
        return rcopy(
            acc.at[k, h], rsb.at[side, j], rss.at[side, j], rrs.at[side, j], (there * NX + x, rep)
        )

    def send_unit(side, j):
        seq = (RIGHT, LEFT)[side]
        dist, h = seq[j]
        if (dist + 1, h) in seq:
            i = seq.index((dist + 1, h))
            k = lax.rem(z + dist, NZ) if side == 0 else lax.rem(z + NZ - dist, NZ)
            unit(side, i).wait_recv()
            acc[k, h] = acc[k, h] + rsb[side, i]
        unit(side, j).start()

    for j in range(2):
        for side in range(2):
            send_unit(side, j)

    @pl.when(d > 0)
    def _():
        g_up.wait_recv()

    @pl.when(d < NX * NZ - 1)
    def _():
        g_down.wait_recv()

    nt = (((1,), (1,)), ((), ()))

    def field_grad(p):
        lhs = jnp.concatenate(
            [
                gbuf[2 + p - kd, (2 - kh) * 16 : (2 - kh) * 16 + 256, :]
                for kd in range(3)
                for kh in range(3)
            ],
            axis=1,
        )
        y = []
        for kw in range(3):
            rhs = jnp.concatenate([wk[b, kw] for b in range(9)], axis=1)
            y.append(lax.dot_general(lhs, rhs, nt, preferred_element_type=F32))
        total = (
            y[1]
            + jnp.where(w_of <= 14, pltpu.roll(y[0], 255, 0), 0.0)
            + jnp.where(w_of >= 1, pltpu.roll(y[2], 1, 0), 0.0)
        )
        gout[p] = total.astype(BF16)

    field_grad(0)
    for side in range(2):
        send_unit(side, 2)
    field_grad(1)
    for j in range(3, 7):
        for side in range(2):
            send_unit(side, j)

    which = lax.broadcasted_iota(jnp.int32, (56, 128), 1) // 32
    for h in range(2):
        rfin[h, 216:224, :] = jnp.zeros((8, 128), F32)

    def owner_copy(q, j):
        return rcopy(
            fsend.at[2 * q + j], frecv.at[rep], fss.at[2 * q + j], frs.at[rep], (z * NX + q, 2 * x + j)
        )

    def owner_local(q, j):
        return pltpu.make_async_copy(fsend.at[2 * q + j], frecv.at[rep], fss.at[2 * q + j])

    for h in (1, 0):
        ir, il = RIGHT.index((1, h)), LEFT.index((1, h))
        unit(0, ir).wait_recv()
        unit(1, il).wait_recv()
        rfin[h, 0:216, :] = (acc[z, h] + rsb[0, ir] + rsb[1, il]) * FACTOR
        for side in range(2):
            q = 2 * side + h
            for j in range(2):
                packed = jnp.zeros((56, 128), F32)
                for m in range(4):
                    part = rfin[h, m * 56 : m * 56 + 56, :]
                    shift = (32 * (m - 2 * side - j)) % 128
                    if shift:
                        part = pltpu.roll(part, shift, 1)
                    packed = jnp.where(which == m, part, packed)
                fsend[2 * q + j] = packed
                here = (x == q) & (rep == 2 * x + j)

                @pl.when(here)
                def _():
                    owner_local(q, j).start()

                @pl.when(jnp.logical_not(here))
                def _():
                    owner_copy(q, j).start()

    for v in range(NR):
        mine = (x == rep // 2) & (rep == v)

        @pl.when(jnp.logical_not(mine))
        def _():
            rcopy(
                fsend.at[v], frecv.at[v], fss.at[v], frs.at[v], (d, lax.rem(rep + 1, NR))
            ).wait_recv()

    for q in range(NX):
        for j in range(2):
            here = (x == q) & (rep == 2 * x + j)

            @pl.when(here)
            def _():
                owner_local(q, j).wait()

            @pl.when(jnp.logical_not(here))
            def _():
                owner_copy(q, j).wait_send()

    lanes = lax.broadcasted_iota(jnp.int32, (8, 128), 1)
    pairs = [(u, v) for u in range(NR) for v in range(u, NR)]
    part = jnp.zeros((8, 128), F32)
    for n, (u, v) in enumerate(pairs):
        prod = frecv[u] * frecv[v]
        total = prod[0:8]
        for m in range(1, 7):
            total = total + prod[8 * m : 8 * m + 8]
        part = jnp.where(lanes == n, jnp.sum(total, axis=1, keepdims=True), part)

    def all_sum(value, index, count, buf, slot, ss, rs, dev):
        gsrc[slot] = value
        buf[index] = value

        def to(i):
            other = lax.rem(index + i, count)
            return rcopy(gsrc.at[slot], buf.at[index], ss.at[i], rs.at[i], dev(other))

        def back(i):
            other = lax.rem(index + count - i, count)
            return rcopy(gsrc.at[slot], buf.at[other], ss.at[i], rs.at[i], dev(other))

        for i in range(1, count):
            to(i).start()
        for i in range(1, count):
            back(i).wait_recv()
        for i in range(1, count):
            to(i).wait_send()
        total = buf[0]
        for i in range(1, count):
            total = total + buf[i]
        return total

    part = all_sum(part, rep, NR, gr1, 0, a1s, a1r, lambda o: (d, o))
    part = all_sum(part, x, NX, gr2, 1, a2s, a2r, lambda o: (z * NX + o, rep))
    part = all_sum(part, z, NZ, gr3, 2, a3s, a3r, lambda o: (o * NX + x, rep))
    whole = jnp.sum(part, axis=0, keepdims=True)
    row = lanes[0:1]
    gram = {
        uv: jnp.sum(jnp.where(row == n, whole, 0.0), axis=1, keepdims=True)
        for n, uv in enumerate(pairs)
    }
    weights = adasum_weights(gram)
    merged = weights[0] * frecv[0]
    for v in range(1, NR):
        merged = merged + weights[v] * frecv[v]
    for m in range(4):
        part = pltpu.roll(merged, 128 - 32 * m, 1) if m else merged
        count = min(56, 216 - 56 * m)
        mout[m * 56 : m * 56 + count, :] = part[0:count, 0:32]

    for p in range(2):
        to_right(p).wait_send()
        to_left(p).wait_send()
    relay_r.wait_send()
    relay_l.wait_send()

    @pl.when((x == 3) & (z < NZ - 1))
    def _():
        up_first.wait_send()

    @pl.when((x == 0) & (z > 0))
    def _():
        down_first.wait_send()

    @pl.when((z < NZ - 1) & (x != 0))
    def _():
        up_last.wait_send()

    @pl.when((z > 0) & (x != 3))
    def _():
        down_last.wait_send()

    for dx in range(1, NX):
        g_send(dx).wait_send()

    @pl.when(d < NX * NZ - 1)
    def _():
        g_up.wait_send()

    @pl.when(d > 0)
    def _():
        g_down.wait_send()

    for side in range(2):
        for j in range(7):
            unit(side, j).wait_send()


def shards(volume, cotangent, kernel_weights):
    dma = pltpu.SemaphoreType.DMA
    any_space = pl.BlockSpec(memory_space=pl.ANY)
    vmem = pl.BlockSpec(memory_space=pltpu.VMEM)
    gout, mout = pl.pallas_call(
        kernel,
        name="adasum_step",
        out_shape=(
            jax.ShapeDtypeStruct((2, 256, 256), BF16),
            jax.ShapeDtypeStruct((216, 32), F32),
        ),
        in_specs=[any_space] * 3,
        out_specs=(vmem, vmem),
        scratch_shapes=[
            pltpu.VMEM((10, 288, 256), BF16),
            pltpu.VMEM((9, 3, 256, 256), BF16),
            pltpu.VMEM((2, 256, 256), BF16),
            pltpu.VMEM((2, 3, 256, 256), F32),
            pltpu.VMEM((4, 288, 256), BF16),
            pltpu.VMEM((4, 64, 512), BF16),
            pltpu.VMEM((4, 64, 512), BF16),
            pltpu.VMEM((256, 2048), BF16),
            pltpu.VMEM((8, 2, 216, 128), F32),
            pltpu.VMEM((2, 7, 216, 128), F32),
            pltpu.VMEM((2, 224, 128), F32),
            pltpu.VMEM((8, 56, 128), F32),
            pltpu.VMEM((8, 56, 128), F32),
            pltpu.VMEM((8, 8, 128), F32),
            pltpu.VMEM((4, 8, 128), F32),
            pltpu.VMEM((8, 8, 128), F32),
            pltpu.VMEM((3, 8, 128), F32),
            dma((4,)),
            dma((10,)), dma((8,)),
            dma((4,)), dma((4,)),
            dma((2,)), dma((2,)),
            dma((2, 7)), dma((2, 7)),
            dma((8,)), dma((8,)),
            dma((8,)), dma((8,)),
            dma((4,)), dma((4,)),
            dma((8,)), dma((8,)),
        ],
        compiler_params=pltpu.CompilerParams(
            collective_id=0, has_side_effects=True, vmem_limit_bytes=56 * 1024 * 1024
        ),
    )(
        volume.reshape(2, 256, 256),
        cotangent.reshape(2, 256, 256),
        kernel_weights.reshape(9, 3, 256, 256),
    )
    return gout.reshape(1, 2, 16, 16, 256), mout


def solution(mesh):
    return jax.shard_map(
        shards,
        mesh=mesh,
        in_specs=(P("replica", "depth"), P("replica", "depth"), P()),
        out_specs=(P("replica", "depth"), P("depth", "replica")),
        check_vma=False,
    )
```

```python
import functools

import jax
import jax.numpy as jnp
from jax import lax
from jax.experimental import pallas as pl
from jax.experimental.pallas import tpu as pltpu
from jax.sharding import PartitionSpec as P

MESH = pl.DeviceIdType.MESH
EPS = 1e-06
F32, BF16 = jnp.float32, jnp.bfloat16
NX, NZ, NR = 4, 8, 8
FACTOR = 1.0 / 128.0

def rcopy(src, dst, ss, rs, dev):
    return pltpu.make_async_remote_copy(
        src_ref=src, dst_ref=dst, send_sem=ss, recv_sem=rs, device_id=dev, device_id_type=MESH
    )


def adasum_weights(gram):
    dots = dict(gram)
    count = NR
    weights = [None] * NR
    members = [[v] for v in range(NR)]
    while count > 1:
        alpha = [None] * count
        for a in range(0, count, 2):
            b = a + 1
            half = 0.5 * dots[(a, b)]
            alpha[a] = 1.0 - half / (jnp.maximum(dots[(a, a)], 0.0) + EPS)
            alpha[b] = 1.0 - half / (jnp.maximum(dots[(b, b)], 0.0) + EPS)
        for a in range(count):
            for v in members[a]:
                weights[v] = alpha[a] if weights[v] is None else weights[v] * alpha[a]
        merged = {}
        half_count = count // 2
        for i in range(half_count):
            for j in range(i, half_count):
                total = None
                for a in (2 * i, 2 * i + 1):
                    for b in (2 * j, 2 * j + 1):
                        term = alpha[a] * alpha[b] * dots[(min(a, b), max(a, b))]
                        total = term if total is None else total + term
                merged[(i, j)] = total
        members = [members[2 * i] + members[2 * i + 1] for i in range(half_count)]
        dots = merged
        count = half_count
    return weights


def kernel(
    vol, cot, kern,
    gout, mout,
    x10, wk, cotv, ybuf, gbuf, gts, gtall, g3, acc, rsb, nsend, nrecv, rfin, fsend, frecv, gr1, gr2, gsrc,
    lsem, rdy, xss, xrs, gss, grs, hss, hrs, rss, rrs, fss, frs, a1s, a1r, a2s, a2r,
):
    d = lax.axis_index("depth")
    rep = lax.axis_index("replica")
    z = d // NX
    x = lax.rem(d, NX)
    xr, xl = lax.rem(x + 1, NX), lax.rem(x + 3, NX)
    xo = lax.rem(x + 2, NX)
    zr, zl = lax.rem(z + 1, NZ), lax.rem(z + 7, NZ)

    sends, expected = [], {}

    def go(copy, cond=None):
        sends.append((copy, cond))
        if cond is None:
            copy.start()
        else:
            pl.when(cond)(copy.start)

    def expect(key, copy, cond=None):
        expected[key] = (copy, cond)

    def got(key):
        copy, cond = expected.pop(key)
        if cond is None:
            copy.wait_recv()
        else:
            pl.when(cond)(copy.wait_recv)

    def finish():
        for key in list(expected):
            got(key)
        for copy, cond in sends:
            if cond is None:
                copy.wait_send()
            else:
                pl.when(cond)(copy.wait_send)

    bar = pltpu.get_barrier_semaphore()

    def greet(dd, rr):
        pl.semaphore_signal(bar, inc=1, device_id=(dd, rr), device_id_type=MESH)

    core = lax.rem(rep, 2)
    near = [
        (d, rep + 1 - 2 * core),
        (d, lax.rem(rep + 2, NR)),
        (d, lax.rem(rep + 6, NR)),
    ]
    for dev in near + [(z * NX + xo, rep), (z * NX + xr, rep), (z * NX + xl, rep), (zr * NX + x, rep), (zl * NX + x, rep)]:
        greet(*dev)

    d_up, d_down = lax.rem(d + 1, NX * NZ), lax.rem(d + NX * NZ - 1, NX * NZ)
    at_top, at_bottom = (x == 3) & (z < NZ - 1), (x == 0) & (z > 0)
    pl.when(at_top)(lambda: greet(d_up, rep))
    pl.when(at_bottom)(lambda: greet(d_down, rep))

    rows = pl.ds(16, 256)
    lx = [pltpu.make_async_copy(vol.at[p], x10.at[1 + 2 * x + p, rows], lsem.at[p]) for p in range(2)]
    lw = pltpu.make_async_copy(kern, wk, lsem.at[2])
    lc = pltpu.make_async_copy(cot, cotv, lsem.at[3])
    for c in lx:
        c.start()
    lw.start()
    lc.start()
    pad = jnp.zeros((16, 256), BF16)
    for k in range(10):
        x10[k, 0:16, :] = pad
        x10[k, 272:288, :] = pad
    for k in range(4):
        gbuf[k, 0:16, :] = pad
        gbuf[k, 272:288, :] = pad

    @pl.when(z == 0)
    def _():
        x10[0, 16:272, :] = jnp.zeros((256, 256), BF16)

    @pl.when(z == NZ - 1)
    def _():
        x10[9, 16:272, :] = jnp.zeros((256, 256), BF16)

    @pl.when(d == 0)
    def _():
        gbuf[0, 16:272, :] = jnp.zeros((256, 256), BF16)

    @pl.when(d == NX * NZ - 1)
    def _():
        gbuf[3, 16:272, :] = jnp.zeros((256, 256), BF16)

    pl.semaphore_wait(bar, 8 + (at_top | at_bottom).astype(jnp.int32))

    dr_, dl_ = z * NX + xr, z * NX + xl

    def plane(owner, p):
        return x10.at[1 + 2 * owner + p, rows]

    def to_right(p):
        return rcopy(vol.at[p], plane(x, p), xss.at[p], xrs.at[p], (dr_, rep))

    def to_left(p):
        return rcopy(vol.at[p], plane(x, p), xss.at[2 + p], xrs.at[2 + p], (dl_, rep))

    def from_left(p):
        return rcopy(vol.at[p], plane(xl, p), xss.at[p], xrs.at[p], (dr_, rep))

    def from_right(p):
        return rcopy(vol.at[p], plane(xr, p), xss.at[2 + p], xrs.at[2 + p], (dl_, rep))

    relay_r = rcopy(plane(xl, 1), plane(xl, 1), xss.at[4], xrs.at[4], (dr_, rep))
    relay_l = rcopy(plane(xr, 0), plane(xr, 0), xss.at[5], xrs.at[5], (dl_, rep))
    from_relay_l = rcopy(plane(xo, 1), plane(xo, 1), xss.at[4], xrs.at[4], (dr_, rep))
    from_relay_r = rcopy(plane(xo, 0), plane(xo, 0), xss.at[5], xrs.at[5], (dl_, rep))

    low, high = x10.at[0, rows], x10.at[9, rows]
    up_first = rcopy(vol.at[1], low, xss.at[6], xrs.at[6], (d_up, rep))
    down_first = rcopy(vol.at[0], high, xss.at[7], xrs.at[7], (d_down, rep))
    up = rcopy(x10.at[8, rows], low, xss.at[8], xrs.at[6], (zr * NX + x, rep))
    down = rcopy(x10.at[1, rows], high, xss.at[9], xrs.at[7], (zl * NX + x, rep))
    is_low, is_high = z > 0, z < NZ - 1

    go(up_first, at_top)
    go(down_first, at_bottom)
    go(to_right(1))
    go(to_left(0))
    go(to_right(0))
    go(to_left(1))
    for dev in ((zr * NX + x, rep), (zl * NX + x, rep)):
        pl.semaphore_signal(rdy.at[3], inc=1, device_id=dev, device_id_type=MESH)
    for c in lx:
        c.wait()
    go(up, is_high & (x == 3))
    go(down, is_low & (x == 0))
    for p in range(2):
        expect(("left", p), from_left(p))
        expect(("right", p), from_right(p))
    expect("low0", up, at_bottom)
    expect("high0", down, at_top)
    expect("low1", up, is_low & (x != 0))
    expect("high1", down, is_high & (x != 3))
    expect("relay_l", from_relay_l)
    expect("relay_r", from_relay_r)

    lw.wait()
    for p in range(2):
        taps = [(kd, kh) for kd in ((1, 2) if p == 0 else (0, 1)) for kh in range(3)]
        lhs = jnp.concatenate(
            [x10[2 * x + p + kd, kh * 16 : kh * 16 + 256, :] for kd, kh in taps], axis=1
        )
        for kw in range(3):
            rhs = jnp.concatenate([wk[kd * 3 + kh, kw] for kd, kh in taps], axis=0)
            ybuf[p, kw] = jnp.dot(lhs, rhs, preferred_element_type=F32)
    lc.wait()

    got(("left", 1))
    go(relay_r)
    got(("right", 0))
    go(relay_l)
    got("low0")
    got("high0")
    w_of = lax.rem(lax.broadcasted_iota(jnp.int32, (256, 256), 0), 16)
    for p in range(2):
        kd = 0 if p == 0 else 2
        lhs = jnp.concatenate(
            [x10[2 * x + p + kd, kh * 16 : kh * 16 + 256, :] for kh in range(3)], axis=1
        )
        y = []
        for kw in range(3):
            rhs = jnp.concatenate([wk[kd * 3 + kh, kw] for kh in range(3)], axis=0)
            y.append(ybuf[p, kw] + jnp.dot(lhs, rhs, preferred_element_type=F32))
        preact = (
            y[1]
            + jnp.where(w_of >= 1, pltpu.roll(y[0], 1, 0), 0.0)
            + jnp.where(w_of <= 14, pltpu.roll(y[2], 255, 0), 0.0)
        )
        s = jax.nn.sigmoid(preact)
        g = (cotv[p].astype(F32) * s * (1.0 + preact * (1.0 - s))).astype(BF16)
        gbuf[1 + p, 16:272, :] = g
        gt = g.astype(F32).T.astype(BF16)
        for q in range(NX):
            gts[q, :, p * 256 : p * 256 + 256] = gt[q * 64 : q * 64 + 64, :]

    def g_send(dx):
        q = lax.rem(x + dx, NX)
        return rcopy(gts.at[q], gtall.at[x], gss.at[dx], grs.at[dx], (z * NX + q, rep))

    def g_recv(dx):
        q = lax.rem(x + NX - dx, NX)
        return rcopy(gts.at[q], gtall.at[q], gss.at[dx], grs.at[dx], (z * NX + q, rep))

    for dx in (2, 1, 3):
        go(g_send(dx))
        expect(("g", dx), g_recv(dx))
    gtall[x] = gts[x]

    got(("left", 0))
    got(("right", 1))
    got("relay_l")
    got("relay_r")
    inner = (x == 1) | (x == 2)
    go(up, is_high & inner)
    go(down, is_low & inner)

    g_up = rcopy(gbuf.at[2, rows], gbuf.at[0, rows], hss.at[0], hrs.at[0], (d_up, rep))
    g_down = rcopy(
        gbuf.at[1, rows], gbuf.at[3, rows], hss.at[1], hrs.at[1], (lax.rem(d + NX * NZ - 1, NX * NZ), rep)
    )
    go(g_up, d < NX * NZ - 1)
    go(g_down, d > 0)
    expect("g_low", g_up, d > 0)
    expect("g_high", g_down, d < NX * NZ - 1)

    for key in (("g", 1), ("g", 3), ("g", 2)):
        got(key)
    lane = lax.rem(lax.broadcasted_iota(jnp.int32, (64, 512), 1), 16)
    for q in range(NX):
        t = gtall[q].astype(F32)
        cols = slice(q * 512, q * 512 + 512)
        g3[0:64, cols] = jnp.where(lane <= 14, pltpu.roll(t, 511, 1), 0.0).astype(BF16)
        g3[64:128, cols] = t.astype(BF16)
        last = jnp.where(lane >= 1, pltpu.roll(t, 1, 1), 0.0).astype(BF16)
        g3[128:192, cols] = last
        g3[192:256, cols] = last


    for b in (3, 4, 5, 0, 1, 2, 6, 7, 8):
        if b == 0:
            got("low1")
            got("high1")
        kd, kh = b // 3, b % 3
        field = x10[kd : kd + 8, kh * 16 : kh * 16 + 256, :].reshape(2048, 256)
        out = jnp.dot(g3[...], field, preferred_element_type=F32).T
        pair, twice = out[:, 0:128], out[:, 128:256]
        swapped = pltpu.roll(pair, 64, 1)
        for kw in range(3):
            start = (3 * b + kw) * 256
            at = start
            while at < start + 256:
                block = at // 216
                end = min(start + 256, (block + 1) * 216)
                k, q = block // 4, block % 4
                side, h = q // 2, q % 2
                source = twice if kw == 2 else (pair if kw == side else swapped)
                acc[k, h, at - block * 216 : end - block * 216, side * 64 : side * 64 + 64] = source[
                    at - start : end - start, side * 64 : side * 64 + 64
                ]
                at = end

    def ready(t):
        for dev in near:
            pl.semaphore_signal(rdy.at[t], inc=1, device_id=dev, device_id_type=MESH)

    half_of = (0, 1)

    def far(side, dist):
        return lax.rem(z + dist, NZ) if side == 0 else lax.rem(z + NZ - dist, NZ)

    hops = {"a": (4, 2), "b": (3, 1), "c": (1, 1), "d": (2, 2)}

    def unit(side, kind, h):
        dist, step = hops[kind]
        there = far(side, step) * NX + x
        if kind == "d":
            src, dst, n = acc.at[far(side, 2), h], rsb.at[side, h], 6 + h
        else:
            n = "abc".index(kind) * 2 + h
            src, dst = nsend.at[side, n], nrecv.at[side, n]
        return rcopy(src, dst, rss.at[side, n], rrs.at[side, n], (there, rep))

    def send_unit(side, kind, h):
        dist, _ = hops[kind]
        k = far(side, dist)
        if kind == "d":
            got(("rs", side, "b", h))
            value = acc[k, h] + nrecv[side, 2 + h].astype(F32)
            if h == half_of[side]:
                got(("rs", side, "a", h))
                value = value + nrecv[side, h].astype(F32)
            acc[k, h] = value
        else:
            nsend[side, "abc".index(kind) * 2 + h] = acc[k, h].astype(BF16)
        go(unit(side, kind, h))
        expect(("rs", side, kind, h), unit(side, kind, h))

    pl.semaphore_wait(rdy.at[3], 2)
    ready(0)
    for side in range(2):
        send_unit(side, "b", 1 - half_of[side])
    for side in range(2):
        send_unit(side, "a", half_of[side])
    for side in range(2):
        send_unit(side, "b", half_of[side])
    for h in range(2):
        for side in range(2):
            send_unit(side, "c", h)

    got("g_low")
    got("g_high")
    nt = (((1,), (1,)), ((), ()))

    def field_grad(p):
        lhs = jnp.concatenate(
            [
                gbuf[2 + p - kd, (2 - kh) * 16 : (2 - kh) * 16 + 256, :]
                for kd in range(3)
                for kh in range(3)
            ],
            axis=1,
        )
        y = []
        for kw in range(3):
            rhs = jnp.concatenate([wk[b, kw] for b in range(9)], axis=1)
            y.append(lax.dot_general(lhs, rhs, nt, preferred_element_type=F32))
        total = (
            y[1]
            + jnp.where(w_of <= 14, pltpu.roll(y[0], 255, 0), 0.0)
            + jnp.where(w_of >= 1, pltpu.roll(y[2], 1, 0), 0.0)
        )
        gout[p] = total.astype(BF16)

    pl.semaphore_wait(rdy.at[0], 3)
    ready(1)
    field_grad(0)
    for side in range(2):
        send_unit(side, "d", 1 - half_of[side])
    for side in range(2):
        send_unit(side, "d", half_of[side])
    pl.semaphore_wait(rdy.at[1], 3)
    ready(2)
    field_grad(1)
    pl.semaphore_wait(rdy.at[2], 3)

    which = lax.broadcasted_iota(jnp.int32, (56, 128), 1) // 32
    for h in range(2):
        rfin[h, 216:224, :] = jnp.zeros((8, 128), F32)

    def owner_copy(q, j):
        return rcopy(
            fsend.at[2 * q + j], frecv.at[rep], fss.at[2 * q + j], frs.at[rep], (z * NX + q, 2 * x + j)
        )

    def owner_local(q, j):
        return pltpu.make_async_copy(fsend.at[2 * q + j], frecv.at[rep], fss.at[2 * q + j])

    for h in (1, 0):
        total = acc[z, h]
        for side in range(2):
            got(("rs", side, "c", h))
            total = total + nrecv[side, 4 + h].astype(F32)
        for side in range(2):
            got(("rs", side, "d", h))
            total = total + rsb[side, h]
        rfin[h, 0:216, :] = total * FACTOR
        for side in range(2):
            q = 2 * side + h
            for j in range(2):
                packed = jnp.zeros((56, 128), F32)
                for m in range(4):
                    part = rfin[h, m * 56 : m * 56 + 56, :]
                    shift = (32 * (m - 2 * side - j)) % 128
                    if shift:
                        part = pltpu.roll(part, shift, 1)
                    packed = jnp.where(which == m, part, packed)
                fsend[2 * q + j] = packed
                here = (x == q) & (rep == 2 * x + j)

                pl.when(here)(owner_local(q, j).start)
                go(owner_copy(q, j), jnp.logical_not(here))

    for v in range(NR):
        mine = (x == rep // 2) & (rep == v)
        copy = rcopy(fsend.at[v], frecv.at[v], fss.at[v], frs.at[v], (d, lax.rem(rep + 1, NR)))
        expect(("own", v), copy, jnp.logical_not(mine))
    for q in range(NX):
        for j in range(2):
            pl.when((x == q) & (rep == 2 * x + j))(owner_local(q, j).wait)
    for v in range(NR):
        got(("own", v))

    lanes = lax.broadcasted_iota(jnp.int32, (8, 128), 1)
    pairs = [(u, v) for u in range(NR) for v in range(u, NR)]
    part = jnp.zeros((8, 128), F32)
    for n, (u, v) in enumerate(pairs):
        prod = frecv[u] * frecv[v]
        total = prod[0:8]
        for m in range(1, 7):
            total = total + prod[8 * m : 8 * m + 8]
        part = jnp.where(lanes == n, jnp.sum(total, axis=1, keepdims=True), part)

    def all_sum(value, index, count, buf, slot, ss, rs, dev):
        gsrc[slot] = value
        buf[index] = value

        def to(i):
            other = lax.rem(index + i, count)
            return rcopy(gsrc.at[slot], buf.at[index], ss.at[i], rs.at[i], dev(other))

        def back(i):
            other = lax.rem(index + count - i, count)
            return rcopy(gsrc.at[slot], buf.at[other], ss.at[i], rs.at[i], dev(other))

        for i in range(1, count):
            go(to(i))
        for i in range(1, count):
            back(i).wait_recv()
        total = buf[0]
        for i in range(1, count):
            total = total + buf[i]
        return total

    part = jnp.sum(part, axis=0, keepdims=True)

    def plane_dev(o):
        return z * NX + o // NR, lax.rem(o, NR)

    part = all_sum(part, x * NR + rep, NX * NR, gr1, 0, a1s, a1r, plane_dev)
    part = all_sum(part, z, NZ, gr2, 1, a2s, a2r, lambda o: (o * NX + x, rep))
    whole = part
    row = lanes[0:1]
    gram = {
        uv: jnp.sum(jnp.where(row == n, whole, 0.0), axis=1, keepdims=True)
        for n, uv in enumerate(pairs)
    }
    weights = adasum_weights(gram)
    merged = weights[0] * frecv[0]
    for v in range(1, NR):
        merged = merged + weights[v] * frecv[v]
    turned = merged.T
    for m in range(4):
        count = min(56, 216 - 56 * m)
        mout[:, m * 56 : m * 56 + count] = turned[m * 32 : m * 32 + 32, 0:count]

    finish()


def hand_over(g, m, g_out, m_out):
    g_out[...] = g[...]
    m_out[...] = m[...]


def shards(volume, cotangent, kernel_weights):
    dma = pltpu.SemaphoreType.DMA
    any_space = pl.BlockSpec(memory_space=pl.ANY)
    vmem = pl.BlockSpec(memory_space=pltpu.VMEM)
    gout, mout = pl.pallas_call(
        kernel,
        name="adasum_step",
        out_shape=(
            jax.ShapeDtypeStruct((2, 256, 256), BF16),
            jax.ShapeDtypeStruct((32, 216), F32),
        ),
        in_specs=[any_space] * 3,
        out_specs=(vmem, vmem),
        scratch_shapes=[
            pltpu.VMEM((10, 288, 256), BF16),
            pltpu.VMEM((9, 3, 256, 256), BF16),
            pltpu.VMEM((2, 256, 256), BF16),
            pltpu.VMEM((2, 3, 256, 256), F32),
            pltpu.VMEM((4, 288, 256), BF16),
            pltpu.VMEM((4, 64, 512), BF16),
            pltpu.VMEM((4, 64, 512), BF16),
            pltpu.VMEM((256, 2048), BF16),
            pltpu.VMEM((8, 2, 216, 128), F32),
            pltpu.VMEM((2, 2, 216, 128), F32),
            pltpu.VMEM((2, 6, 216, 128), BF16),
            pltpu.VMEM((2, 6, 216, 128), BF16),
            pltpu.VMEM((2, 224, 128), F32),
            pltpu.VMEM((8, 56, 128), F32),
            pltpu.VMEM((8, 56, 128), F32),
            pltpu.VMEM((32, 1, 128), F32),
            pltpu.VMEM((8, 1, 128), F32),
            pltpu.VMEM((2, 1, 128), F32),
            dma((4,)),
            pltpu.SemaphoreType.REGULAR((4,)),
            dma((10,)), dma((8,)),
            dma((4,)), dma((4,)),
            dma((2,)), dma((2,)),
            dma((2, 8)), dma((2, 8)),
            dma((8,)), dma((8,)),
            dma((32,)), dma((32,)),
            dma((8,)), dma((8,)),
        ],
        compiler_params=pltpu.CompilerParams(
            collective_id=0, has_side_effects=True, vmem_limit_bytes=56 * 1024 * 1024
        ),
    )(
        volume.reshape(2, 256, 256),
        cotangent.reshape(2, 256, 256),
        kernel_weights.reshape(9, 3, 256, 256),
    )
    gout, mout = pl.pallas_call(
        hand_over,
        name="hand_over",
        out_shape=(
            jax.ShapeDtypeStruct((2, 256, 256), BF16),
            jax.ShapeDtypeStruct((32, 216), F32),
        ),
        in_specs=[vmem] * 2,
        out_specs=(vmem, vmem),
    )(gout, mout)
    return gout.reshape(1, 2, 16, 16, 256), mout.T


def solution(mesh):
    return jax.shard_map(
        shards,
        mesh=mesh,
        in_specs=(P("replica", "depth"), P("replica", "depth"), P()),
        out_specs=(P("replica", "depth"), P("depth", "replica")),
        check_vma=False,
    )
```

```python
import functools

import jax
import jax.numpy as jnp
from jax import lax
from jax.experimental import pallas as pl
from jax.experimental.pallas import tpu as pltpu
from jax.sharding import PartitionSpec as P

MESH = pl.DeviceIdType.MESH
EPS = 1e-06
F32, BF16 = jnp.float32, jnp.bfloat16
NX, NZ, NR = 4, 8, 8
FACTOR = 1.0 / 128.0

def rcopy(src, dst, ss, rs, dev):
    return pltpu.make_async_remote_copy(
        src_ref=src, dst_ref=dst, send_sem=ss, recv_sem=rs, device_id=dev, device_id_type=MESH
    )


def adasum_weights(gram):
    dots = dict(gram)
    count = NR
    weights = [None] * NR
    members = [[v] for v in range(NR)]
    while count > 1:
        alpha = [None] * count
        for a in range(0, count, 2):
            b = a + 1
            half = 0.5 * dots[(a, b)]
            alpha[a] = 1.0 - half / (jnp.maximum(dots[(a, a)], 0.0) + EPS)
            alpha[b] = 1.0 - half / (jnp.maximum(dots[(b, b)], 0.0) + EPS)
        for a in range(count):
            for v in members[a]:
                weights[v] = alpha[a] if weights[v] is None else weights[v] * alpha[a]
        merged = {}
        half_count = count // 2
        for i in range(half_count):
            for j in range(i, half_count):
                total = None
                for a in (2 * i, 2 * i + 1):
                    for b in (2 * j, 2 * j + 1):
                        term = alpha[a] * alpha[b] * dots[(min(a, b), max(a, b))]
                        total = term if total is None else total + term
                merged[(i, j)] = total
        members = [members[2 * i] + members[2 * i + 1] for i in range(half_count)]
        dots = merged
        count = half_count
    return weights


def kernel(
    vol, cot, kern,
    gout, mout,
    x10, wk, cotv, ybuf, gbuf, gts, gtall, g3, acc, rsb, nsend, nrecv, rfin, fsend, frecv, gr1, gr2, gsrc,
    lsem, rdy, xss, xrs, gss, grs, hss, hrs, rss, rrs, fss, frs, a1s, a1r, a2s, a2r,
):
    d = lax.axis_index("depth")
    rep = lax.axis_index("replica")
    z = d // NX
    x = lax.rem(d, NX)
    xr, xl = lax.rem(x + 1, NX), lax.rem(x + 3, NX)
    xo = lax.rem(x + 2, NX)
    zr, zl = lax.rem(z + 1, NZ), lax.rem(z + 7, NZ)

    sends, expected = [], {}

    def go(copy, cond=None):
        sends.append((copy, cond))
        if cond is None:
            copy.start()
        else:
            pl.when(cond)(copy.start)

    def expect(key, copy, cond=None):
        expected[key] = (copy, cond)

    def got(key):
        copy, cond = expected.pop(key)
        if cond is None:
            copy.wait_recv()
        else:
            pl.when(cond)(copy.wait_recv)

    def finish():
        for key in list(expected):
            got(key)
        for copy, cond in sends:
            if cond is None:
                copy.wait_send()
            else:
                pl.when(cond)(copy.wait_send)

    bar = pltpu.get_barrier_semaphore()

    def greet(dd, rr):
        pl.semaphore_signal(bar, inc=1, device_id=(dd, rr), device_id_type=MESH)

    core = lax.rem(rep, 2)
    near = [
        (d, rep + 1 - 2 * core),
        (d, lax.rem(rep + 2, NR)),
        (d, lax.rem(rep + 6, NR)),
    ]
    for dev in near + [(z * NX + xo, rep), (z * NX + xr, rep), (z * NX + xl, rep), (zr * NX + x, rep), (zl * NX + x, rep)]:
        greet(*dev)

    d_up, d_down = lax.rem(d + 1, NX * NZ), lax.rem(d + NX * NZ - 1, NX * NZ)
    at_top, at_bottom = (x == 3) & (z < NZ - 1), (x == 0) & (z > 0)
    pl.when(at_top)(lambda: greet(d_up, rep))
    pl.when(at_bottom)(lambda: greet(d_down, rep))

    rows = pl.ds(16, 256)
    lx = [pltpu.make_async_copy(vol.at[p], x10.at[1 + 2 * x + p, rows], lsem.at[p]) for p in range(2)]
    lw = pltpu.make_async_copy(kern, wk, lsem.at[2])
    lc = pltpu.make_async_copy(cot, cotv, lsem.at[3])
    for c in lx:
        c.start()
    lw.start()
    lc.start()
    pad = jnp.zeros((16, 256), BF16)
    for k in range(10):
        x10[k, 0:16, :] = pad
        x10[k, 272:288, :] = pad
    for k in range(4):
        gbuf[k, 0:16, :] = pad
        gbuf[k, 272:288, :] = pad

    @pl.when(z == 0)
    def _():
        x10[0, 16:272, :] = jnp.zeros((256, 256), BF16)

    @pl.when(z == NZ - 1)
    def _():
        x10[9, 16:272, :] = jnp.zeros((256, 256), BF16)

    @pl.when(d == 0)
    def _():
        gbuf[0, 16:272, :] = jnp.zeros((256, 256), BF16)

    @pl.when(d == NX * NZ - 1)
    def _():
        gbuf[3, 16:272, :] = jnp.zeros((256, 256), BF16)

    pl.semaphore_wait(bar, 8 + (at_top | at_bottom).astype(jnp.int32))

    dr_, dl_ = z * NX + xr, z * NX + xl

    def plane(owner, p):
        return x10.at[1 + 2 * owner + p, rows]

    def to_right(p):
        return rcopy(vol.at[p], plane(x, p), xss.at[p], xrs.at[p], (dr_, rep))

    def to_left(p):
        return rcopy(vol.at[p], plane(x, p), xss.at[2 + p], xrs.at[2 + p], (dl_, rep))

    def from_left(p):
        return rcopy(vol.at[p], plane(xl, p), xss.at[p], xrs.at[p], (dr_, rep))

    def from_right(p):
        return rcopy(vol.at[p], plane(xr, p), xss.at[2 + p], xrs.at[2 + p], (dl_, rep))

    relay_r = rcopy(plane(xl, 1), plane(xl, 1), xss.at[4], xrs.at[4], (dr_, rep))
    relay_l = rcopy(plane(xr, 0), plane(xr, 0), xss.at[5], xrs.at[5], (dl_, rep))
    from_relay_l = rcopy(plane(xo, 1), plane(xo, 1), xss.at[4], xrs.at[4], (dr_, rep))
    from_relay_r = rcopy(plane(xo, 0), plane(xo, 0), xss.at[5], xrs.at[5], (dl_, rep))

    low, high = x10.at[0, rows], x10.at[9, rows]
    up_first = rcopy(vol.at[1], low, xss.at[6], xrs.at[6], (d_up, rep))
    down_first = rcopy(vol.at[0], high, xss.at[7], xrs.at[7], (d_down, rep))
    up = rcopy(x10.at[8, rows], low, xss.at[8], xrs.at[6], (zr * NX + x, rep))
    down = rcopy(x10.at[1, rows], high, xss.at[9], xrs.at[7], (zl * NX + x, rep))
    is_low, is_high = z > 0, z < NZ - 1

    go(up_first, at_top)
    go(down_first, at_bottom)
    go(to_right(1))
    go(to_left(0))
    go(to_right(0))
    go(to_left(1))
    for dev in ((zr * NX + x, rep), (zl * NX + x, rep)):
        pl.semaphore_signal(rdy.at[3], inc=1, device_id=dev, device_id_type=MESH)
    for c in lx:
        c.wait()
    go(up, is_high & (x == 3))
    go(down, is_low & (x == 0))
    for p in range(2):
        expect(("left", p), from_left(p))
        expect(("right", p), from_right(p))
    expect("low0", up, at_bottom)
    expect("high0", down, at_top)
    expect("low1", up, is_low & (x != 0))
    expect("high1", down, is_high & (x != 3))
    expect("relay_l", from_relay_l)
    expect("relay_r", from_relay_r)

    lw.wait()
    for p in range(2):
        taps = [(kd, kh) for kd in ((1, 2) if p == 0 else (0, 1)) for kh in range(3)]
        lhs = jnp.concatenate(
            [x10[2 * x + p + kd, kh * 16 : kh * 16 + 256, :] for kd, kh in taps], axis=1
        )
        for kw in range(3):
            rhs = jnp.concatenate([wk[kd * 3 + kh, kw] for kd, kh in taps], axis=0)
            ybuf[p, kw] = jnp.dot(lhs, rhs, preferred_element_type=F32)
    lc.wait()

    got(("left", 1))
    go(relay_r)
    got(("right", 0))
    go(relay_l)
    got("low0")
    got("high0")
    w_of = lax.rem(lax.broadcasted_iota(jnp.int32, (256, 256), 0), 16)
    for p in range(2):
        kd = 0 if p == 0 else 2
        lhs = jnp.concatenate(
            [x10[2 * x + p + kd, kh * 16 : kh * 16 + 256, :] for kh in range(3)], axis=1
        )
        y = []
        for kw in range(3):
            rhs = jnp.concatenate([wk[kd * 3 + kh, kw] for kh in range(3)], axis=0)
            y.append(ybuf[p, kw] + jnp.dot(lhs, rhs, preferred_element_type=F32))
        preact = (
            y[1]
            + jnp.where(w_of >= 1, pltpu.roll(y[0], 1, 0), 0.0)
            + jnp.where(w_of <= 14, pltpu.roll(y[2], 255, 0), 0.0)
        )
        s = jax.nn.sigmoid(preact)
        g = (cotv[p].astype(F32) * s * (1.0 + preact * (1.0 - s))).astype(BF16)
        gbuf[1 + p, 16:272, :] = g
        gt = g.astype(F32).T.astype(BF16)
        for q in range(NX):
            gts[q, :, p * 256 : p * 256 + 256] = gt[q * 64 : q * 64 + 64, :]

    def g_send(dx):
        q = lax.rem(x + dx, NX)
        return rcopy(gts.at[q], gtall.at[x], gss.at[dx], grs.at[dx], (z * NX + q, rep))

    def g_recv(dx):
        q = lax.rem(x + NX - dx, NX)
        return rcopy(gts.at[q], gtall.at[q], gss.at[dx], grs.at[dx], (z * NX + q, rep))

    for dx in (2, 1, 3):
        go(g_send(dx))
        expect(("g", dx), g_recv(dx))
    gtall[x] = gts[x]

    got(("left", 0))
    got(("right", 1))
    got("relay_l")
    got("relay_r")
    inner = (x == 1) | (x == 2)
    go(up, is_high & inner)
    go(down, is_low & inner)

    g_up = rcopy(gbuf.at[2, rows], gbuf.at[0, rows], hss.at[0], hrs.at[0], (d_up, rep))
    g_down = rcopy(
        gbuf.at[1, rows], gbuf.at[3, rows], hss.at[1], hrs.at[1], (lax.rem(d + NX * NZ - 1, NX * NZ), rep)
    )
    go(g_up, d < NX * NZ - 1)
    go(g_down, d > 0)
    expect("g_low", g_up, d > 0)
    expect("g_high", g_down, d < NX * NZ - 1)

    for key in (("g", 1), ("g", 3), ("g", 2)):
        got(key)
    lane = lax.rem(lax.broadcasted_iota(jnp.int32, (64, 512), 1), 16)
    for q in range(NX):
        t = gtall[q].astype(F32)
        cols = slice(q * 512, q * 512 + 512)
        g3[0:64, cols] = jnp.where(lane <= 14, pltpu.roll(t, 511, 1), 0.0).astype(BF16)
        g3[64:128, cols] = t.astype(BF16)
        last = jnp.where(lane >= 1, pltpu.roll(t, 1, 1), 0.0).astype(BF16)
        g3[128:192, cols] = last
        g3[192:256, cols] = last


    for b in (3, 4, 5, 0, 1, 2, 6, 7, 8):
        if b == 0:
            got("low1")
            got("high1")
        kd, kh = b // 3, b % 3
        field = x10[kd : kd + 8, kh * 16 : kh * 16 + 256, :].reshape(2048, 256)
        out = jnp.dot(g3[...], field, preferred_element_type=F32).T
        pair, twice = out[:, 0:128], out[:, 128:256]
        swapped = pltpu.roll(pair, 64, 1)
        for kw in range(3):
            start = (3 * b + kw) * 256
            at = start
            while at < start + 256:
                block = at // 216
                end = min(start + 256, (block + 1) * 216)
                k, q = block // 4, block % 4
                side, h = q // 2, q % 2
                source = twice if kw == 2 else (pair if kw == side else swapped)
                acc[k, h, at - block * 216 : end - block * 216, side * 64 : side * 64 + 64] = source[
                    at - start : end - start, side * 64 : side * 64 + 64
                ]
                at = end

    def ready(t):
        for dev in near:
            pl.semaphore_signal(rdy.at[t], inc=1, device_id=dev, device_id_type=MESH)

    half_of = (0, 1)

    def far(side, dist):
        return lax.rem(z + dist, NZ) if side == 0 else lax.rem(z + NZ - dist, NZ)

    hops = {"a": (4, 2), "b": (3, 1), "c": (1, 1), "d": (2, 2)}

    def unit(side, kind, h):
        dist, step = hops[kind]
        there = far(side, step) * NX + x
        if kind == "d":
            src, dst, n = acc.at[far(side, 2), h], rsb.at[side, h], 6 + h
        else:
            n = "abc".index(kind) * 2 + h
            src, dst = nsend.at[side, n], nrecv.at[side, n]
        return rcopy(src, dst, rss.at[side, n], rrs.at[side, n], (there, rep))

    def send_unit(side, kind, h):
        dist, _ = hops[kind]
        k = far(side, dist)
        if kind == "d":
            got(("rs", side, "b", h))
            value = acc[k, h] + nrecv[side, 2 + h].astype(F32)
            if h == half_of[side]:
                got(("rs", side, "a", h))
                value = value + nrecv[side, h].astype(F32)
            acc[k, h] = value
        else:
            nsend[side, "abc".index(kind) * 2 + h] = acc[k, h].astype(BF16)
        go(unit(side, kind, h))
        expect(("rs", side, kind, h), unit(side, kind, h))

    pl.semaphore_wait(rdy.at[3], 2)
    ready(0)
    for side in range(2):
        send_unit(side, "a", half_of[side])
    for kind in ("b", "c"):
        for h in (1, 0):
            for side in range(2):
                send_unit(side, kind, h)

    got("g_low")
    got("g_high")
    nt = (((1,), (1,)), ((), ()))

    def field_grad(p):
        lhs = jnp.concatenate(
            [
                gbuf[2 + p - kd, (2 - kh) * 16 : (2 - kh) * 16 + 256, :]
                for kd in range(3)
                for kh in range(3)
            ],
            axis=1,
        )
        y = []
        for kw in range(3):
            rhs = jnp.concatenate([wk[b, kw] for b in range(9)], axis=1)
            y.append(lax.dot_general(lhs, rhs, nt, preferred_element_type=F32))
        total = (
            y[1]
            + jnp.where(w_of <= 14, pltpu.roll(y[0], 255, 0), 0.0)
            + jnp.where(w_of >= 1, pltpu.roll(y[2], 1, 0), 0.0)
        )
        gout[p] = total.astype(BF16)

    pl.semaphore_wait(rdy.at[0], 3)
    ready(1)
    field_grad(0)
    for side in range(2):
        send_unit(side, "d", 1)
    for side in range(2):
        send_unit(side, "d", 0)
    pl.semaphore_wait(rdy.at[1], 3)
    ready(2)
    field_grad(1)
    pl.semaphore_wait(rdy.at[2], 3)

    which = lax.broadcasted_iota(jnp.int32, (56, 128), 1) // 32
    for h in range(2):
        rfin[h, 216:224, :] = jnp.zeros((8, 128), F32)

    def owner_copy(q, j):
        return rcopy(
            fsend.at[2 * q + j], frecv.at[rep], fss.at[2 * q + j], frs.at[rep], (z * NX + q, 2 * x + j)
        )

    def owner_local(q, j):
        return pltpu.make_async_copy(fsend.at[2 * q + j], frecv.at[rep], fss.at[2 * q + j])

    for h in (1, 0):
        total = acc[z, h]
        for side in range(2):
            got(("rs", side, "c", h))
            total = total + nrecv[side, 4 + h].astype(F32)
        for side in range(2):
            got(("rs", side, "d", h))
            total = total + rsb[side, h]
        rfin[h, 0:216, :] = total * FACTOR
        for side in range(2):
            q = 2 * side + h
            for j in range(2):
                packed = jnp.zeros((56, 128), F32)
                for m in range(4):
                    part = rfin[h, m * 56 : m * 56 + 56, :]
                    shift = (32 * (m - 2 * side - j)) % 128
                    if shift:
                        part = pltpu.roll(part, shift, 1)
                    packed = jnp.where(which == m, part, packed)
                fsend[2 * q + j] = packed
                here = (x == q) & (rep == 2 * x + j)

                pl.when(here)(owner_local(q, j).start)
                go(owner_copy(q, j), jnp.logical_not(here))

    for v in range(NR):
        mine = (x == rep // 2) & (rep == v)
        copy = rcopy(fsend.at[v], frecv.at[v], fss.at[v], frs.at[v], (d, lax.rem(rep + 1, NR)))
        expect(("own", v), copy, jnp.logical_not(mine))
    for q in range(NX):
        for j in range(2):
            pl.when((x == q) & (rep == 2 * x + j))(owner_local(q, j).wait)
    for v in range(NR):
        got(("own", v))

    lanes = lax.broadcasted_iota(jnp.int32, (8, 128), 1)
    pairs = [(u, v) for u in range(NR) for v in range(u, NR)]
    part = jnp.zeros((8, 128), F32)
    for n, (u, v) in enumerate(pairs):
        prod = frecv[u] * frecv[v]
        total = prod[0:8]
        for m in range(1, 7):
            total = total + prod[8 * m : 8 * m + 8]
        part = jnp.where(lanes == n, jnp.sum(total, axis=1, keepdims=True), part)

    part = jnp.sum(part, axis=0, keepdims=True)

    gsrc[0] = part
    partner = rcopy(gsrc.at[0], gr1.at[0], a1s.at[0], a1r.at[0], near[0])
    go(partner)
    expect("partner", partner)
    got("partner")
    part = part + gr1[0]
    gsrc[1] = part
    chips = NX * NZ * NR // 2
    chip = d * (NR // 2) + rep // 2
    gr2[chip] = part

    def tell(i, _):
        other = lax.rem(chip + i, chips)
        dev = (other // (NR // 2), lax.rem(other, NR // 2) * 2 + core)
        rcopy(gsrc.at[1], gr2.at[chip], a2s.at[0], a2r.at[0], dev).start()
        return 0

    lax.fori_loop(1, chips, tell, 0)
    rest = gr2.at[pl.ds(0, chips - 1)]
    told = rcopy(rest, rest, a2s.at[0], a2r.at[0], near[0])
    told.wait_recv()
    told.wait_send()
    part = jnp.sum(gr2[...], axis=0)
    whole = part
    row = lanes[0:1]
    gram = {
        uv: jnp.sum(jnp.where(row == n, whole, 0.0), axis=1, keepdims=True)
        for n, uv in enumerate(pairs)
    }
    weights = adasum_weights(gram)
    merged = weights[0] * frecv[0]
    for v in range(1, NR):
        merged = merged + weights[v] * frecv[v]
    turned = merged.T
    for m in range(4):
        count = min(56, 216 - 56 * m)
        mout[:, m * 56 : m * 56 + count] = turned[m * 32 : m * 32 + 32, 0:count]

    finish()


def shards(volume, cotangent, kernel_weights):
    dma = pltpu.SemaphoreType.DMA
    any_space = pl.BlockSpec(memory_space=pl.ANY)
    vmem = pl.BlockSpec(memory_space=pltpu.VMEM)
    gout, mout = pl.pallas_call(
        kernel,
        name="adasum_step",
        out_shape=(
            pltpu.VMEM((2, 256, 256), BF16),
            pltpu.VMEM((32, 216), F32),
        ),
        in_specs=[any_space] * 3,
        out_specs=(vmem, vmem),
        scratch_shapes=[
            pltpu.VMEM((10, 288, 256), BF16),
            pltpu.VMEM((9, 3, 256, 256), BF16),
            pltpu.VMEM((2, 256, 256), BF16),
            pltpu.VMEM((2, 3, 256, 256), F32),
            pltpu.VMEM((4, 288, 256), BF16),
            pltpu.VMEM((4, 64, 512), BF16),
            pltpu.VMEM((4, 64, 512), BF16),
            pltpu.VMEM((256, 2048), BF16),
            pltpu.VMEM((8, 2, 216, 128), F32),
            pltpu.VMEM((2, 2, 216, 128), F32),
            pltpu.VMEM((2, 6, 216, 128), BF16),
            pltpu.VMEM((2, 6, 216, 128), BF16),
            pltpu.VMEM((2, 224, 128), F32),
            pltpu.VMEM((8, 56, 128), F32),
            pltpu.VMEM((8, 56, 128), F32),
            pltpu.VMEM((1, 1, 128), F32),
            pltpu.VMEM((128, 1, 128), F32),
            pltpu.VMEM((2, 1, 128), F32),
            dma((4,)),
            pltpu.SemaphoreType.REGULAR((4,)),
            dma((10,)), dma((8,)),
            dma((4,)), dma((4,)),
            dma((2,)), dma((2,)),
            dma((2, 8)), dma((2, 8)),
            dma((8,)), dma((8,)),
            dma((1,)), dma((1,)),
            dma((1,)), dma((1,)),
        ],
        compiler_params=pltpu.CompilerParams(
            collective_id=0, has_side_effects=True, vmem_limit_bytes=56 * 1024 * 1024
        ),
    )(
        volume.reshape(2, 256, 256),
        cotangent.reshape(2, 256, 256),
        kernel_weights.reshape(9, 3, 256, 256),
    )
    return gout.reshape(1, 2, 16, 16, 256), mout.T


def solution(mesh):
    return jax.shard_map(
        shards,
        mesh=mesh,
        in_specs=(P("replica", "depth"), P("replica", "depth"), P()),
        out_specs=(P("replica", "depth"), P("depth", "replica")),
        check_vma=False,
    )
```

```python
import functools

import jax
import jax.numpy as jnp
from jax import lax
from jax.experimental import pallas as pl
from jax.experimental.pallas import tpu as pltpu
from jax.sharding import PartitionSpec as P

MESH = pl.DeviceIdType.MESH
EPS = 1e-06
F32, BF16 = jnp.float32, jnp.bfloat16
NX, NZ, NR = 4, 8, 8
FACTOR = 1.0 / 128.0

def rcopy(src, dst, ss, rs, dev):
    return pltpu.make_async_remote_copy(
        src_ref=src, dst_ref=dst, send_sem=ss, recv_sem=rs, device_id=dev, device_id_type=MESH
    )


def adasum_weights(gram):
    dots = dict(gram)
    count = NR
    weights = [None] * NR
    members = [[v] for v in range(NR)]
    while count > 1:
        alpha = [None] * count
        for a in range(0, count, 2):
            b = a + 1
            half = 0.5 * dots[(a, b)]
            alpha[a] = 1.0 - half / (jnp.maximum(dots[(a, a)], 0.0) + EPS)
            alpha[b] = 1.0 - half / (jnp.maximum(dots[(b, b)], 0.0) + EPS)
        for a in range(count):
            for v in members[a]:
                weights[v] = alpha[a] if weights[v] is None else weights[v] * alpha[a]
        merged = {}
        half_count = count // 2
        for i in range(half_count):
            for j in range(i, half_count):
                total = None
                for a in (2 * i, 2 * i + 1):
                    for b in (2 * j, 2 * j + 1):
                        term = alpha[a] * alpha[b] * dots[(min(a, b), max(a, b))]
                        total = term if total is None else total + term
                merged[(i, j)] = total
        members = [members[2 * i] + members[2 * i + 1] for i in range(half_count)]
        dots = merged
        count = half_count
    return weights


def kernel(
    vol, cot, kern,
    gout, mout,
    x10, wk, cotv, ybuf, gbuf, gts, gtall, g3, acc, rsb, nsend, nrecv, rfin, fsend, frecv, gr1, gr2, gsrc,
    lsem, rdy, xss, xrs, gss, grs, hss, hrs, rss, rrs, fss, frs, a1s, a1r, a2s, a2r,
):
    d = lax.axis_index("depth")
    rep = lax.axis_index("replica")
    z = d // NX
    x = lax.rem(d, NX)
    xr, xl = lax.rem(x + 1, NX), lax.rem(x + 3, NX)
    xo = lax.rem(x + 2, NX)
    zr, zl = lax.rem(z + 1, NZ), lax.rem(z + 7, NZ)

    sends, expected = [], {}

    def go(copy, cond=None):
        sends.append((copy, cond))
        if cond is None:
            copy.start()
        else:
            pl.when(cond)(copy.start)

    def expect(key, copy, cond=None):
        expected[key] = (copy, cond)

    def got(key):
        copy, cond = expected.pop(key)
        if cond is None:
            copy.wait_recv()
        else:
            pl.when(cond)(copy.wait_recv)

    def finish():
        for key in list(expected):
            got(key)
        for copy, cond in sends:
            if cond is None:
                copy.wait_send()
            else:
                pl.when(cond)(copy.wait_send)

    bar = pltpu.get_barrier_semaphore()

    def greet(dd, rr):
        pl.semaphore_signal(bar, inc=1, device_id=(dd, rr), device_id_type=MESH)

    core = lax.rem(rep, 2)
    near = [
        (d, rep + 1 - 2 * core),
        (d, lax.rem(rep + 2, NR)),
        (d, lax.rem(rep + 6, NR)),
    ]
    for dev in near + [(z * NX + xo, rep), (z * NX + xr, rep), (z * NX + xl, rep), (zr * NX + x, rep), (zl * NX + x, rep)]:
        greet(*dev)

    d_up, d_down = lax.rem(d + 1, NX * NZ), lax.rem(d + NX * NZ - 1, NX * NZ)
    at_top, at_bottom = (x == 3) & (z < NZ - 1), (x == 0) & (z > 0)
    pl.when(at_top)(lambda: greet(d_up, rep))
    pl.when(at_bottom)(lambda: greet(d_down, rep))

    rows = pl.ds(16, 256)
    lx = [pltpu.make_async_copy(vol.at[p], x10.at[1 + 2 * x + p, rows], lsem.at[p]) for p in range(2)]
    lw = pltpu.make_async_copy(kern, wk, lsem.at[2])
    lc = pltpu.make_async_copy(cot, cotv, lsem.at[3])
    for c in lx:
        c.start()
    lw.start()
    lc.start()
    pad = jnp.zeros((16, 256), BF16)
    for k in range(10):
        x10[k, 0:16, :] = pad
        x10[k, 272:288, :] = pad
    for k in range(4):
        gbuf[k, 0:16, :] = pad
        gbuf[k, 272:288, :] = pad

    @pl.when(z == 0)
    def _():
        x10[0, 16:272, :] = jnp.zeros((256, 256), BF16)

    @pl.when(z == NZ - 1)
    def _():
        x10[9, 16:272, :] = jnp.zeros((256, 256), BF16)

    @pl.when(d == 0)
    def _():
        gbuf[0, 16:272, :] = jnp.zeros((256, 256), BF16)

    @pl.when(d == NX * NZ - 1)
    def _():
        gbuf[3, 16:272, :] = jnp.zeros((256, 256), BF16)

    pl.semaphore_wait(bar, 8 + (at_top | at_bottom).astype(jnp.int32))

    dr_, dl_ = z * NX + xr, z * NX + xl

    def plane(owner, p):
        return x10.at[1 + 2 * owner + p, rows]

    def to_right(p):
        return rcopy(vol.at[p], plane(x, p), xss.at[p], xrs.at[p], (dr_, rep))

    def to_left(p):
        return rcopy(vol.at[p], plane(x, p), xss.at[2 + p], xrs.at[2 + p], (dl_, rep))

    def from_left(p):
        return rcopy(vol.at[p], plane(xl, p), xss.at[p], xrs.at[p], (dr_, rep))

    def from_right(p):
        return rcopy(vol.at[p], plane(xr, p), xss.at[2 + p], xrs.at[2 + p], (dl_, rep))

    relay_r = rcopy(plane(xl, 1), plane(xl, 1), xss.at[4], xrs.at[4], (dr_, rep))
    relay_l = rcopy(plane(xr, 0), plane(xr, 0), xss.at[5], xrs.at[5], (dl_, rep))
    from_relay_l = rcopy(plane(xo, 1), plane(xo, 1), xss.at[4], xrs.at[4], (dr_, rep))
    from_relay_r = rcopy(plane(xo, 0), plane(xo, 0), xss.at[5], xrs.at[5], (dl_, rep))

    low, high = x10.at[0, rows], x10.at[9, rows]
    up_first = rcopy(vol.at[1], low, xss.at[6], xrs.at[6], (d_up, rep))
    down_first = rcopy(vol.at[0], high, xss.at[7], xrs.at[7], (d_down, rep))
    up = rcopy(x10.at[8, rows], low, xss.at[8], xrs.at[6], (zr * NX + x, rep))
    down = rcopy(x10.at[1, rows], high, xss.at[9], xrs.at[7], (zl * NX + x, rep))
    is_low, is_high = z > 0, z < NZ - 1

    go(up_first, at_top)
    go(down_first, at_bottom)
    go(to_right(1))
    go(to_left(0))
    go(to_right(0))
    go(to_left(1))
    for dev in ((zr * NX + x, rep), (zl * NX + x, rep)):
        pl.semaphore_signal(rdy.at[3], inc=1, device_id=dev, device_id_type=MESH)
    for c in lx:
        c.wait()
    go(up, is_high & (x == 3))
    go(down, is_low & (x == 0))
    for p in range(2):
        expect(("left", p), from_left(p))
        expect(("right", p), from_right(p))
    expect("low0", up, at_bottom)
    expect("high0", down, at_top)
    expect("low1", up, is_low & (x != 0))
    expect("high1", down, is_high & (x != 3))
    expect("relay_l", from_relay_l)
    expect("relay_r", from_relay_r)

    lw.wait()
    for p in range(2):
        taps = [(kd, kh) for kd in ((1, 2) if p == 0 else (0, 1)) for kh in range(3)]
        lhs = jnp.concatenate(
            [x10[2 * x + p + kd, kh * 16 : kh * 16 + 256, :] for kd, kh in taps], axis=1
        )
        for kw in range(3):
            rhs = jnp.concatenate([wk[kd * 3 + kh, kw] for kd, kh in taps], axis=0)
            ybuf[p, kw] = jnp.dot(lhs, rhs, preferred_element_type=F32)
    lc.wait()

    got(("left", 1))
    go(relay_r)
    got(("right", 0))
    go(relay_l)
    got("low0")
    got("high0")
    w_of = lax.rem(lax.broadcasted_iota(jnp.int32, (256, 256), 0), 16)
    for p in range(2):
        kd = 0 if p == 0 else 2
        lhs = jnp.concatenate(
            [x10[2 * x + p + kd, kh * 16 : kh * 16 + 256, :] for kh in range(3)], axis=1
        )
        y = []
        for kw in range(3):
            rhs = jnp.concatenate([wk[kd * 3 + kh, kw] for kh in range(3)], axis=0)
            y.append(ybuf[p, kw] + jnp.dot(lhs, rhs, preferred_element_type=F32))
        preact = (
            y[1]
            + jnp.where(w_of >= 1, pltpu.roll(y[0], 1, 0), 0.0)
            + jnp.where(w_of <= 14, pltpu.roll(y[2], 255, 0), 0.0)
        )
        s = jax.nn.sigmoid(preact)
        g = (cotv[p].astype(F32) * s * (1.0 + preact * (1.0 - s))).astype(BF16)
        gbuf[1 + p, 16:272, :] = g
        gt = g.astype(F32).T.astype(BF16)
        for q in range(NX):
            gts[q, :, p * 256 : p * 256 + 256] = gt[q * 64 : q * 64 + 64, :]

    def g_send(dx):
        q = lax.rem(x + dx, NX)
        return rcopy(gts.at[q], gtall.at[x], gss.at[dx], grs.at[dx], (z * NX + q, rep))

    def g_recv(dx):
        q = lax.rem(x + NX - dx, NX)
        return rcopy(gts.at[q], gtall.at[q], gss.at[dx], grs.at[dx], (z * NX + q, rep))

    for dx in (2, 1, 3):
        go(g_send(dx))
        expect(("g", dx), g_recv(dx))
    gtall[x] = gts[x]

    got(("left", 0))
    got(("right", 1))
    got("relay_l")
    got("relay_r")
    inner = (x == 1) | (x == 2)
    go(up, is_high & inner)
    go(down, is_low & inner)
    pl.semaphore_wait(rdy.at[3], 2)
    for dev in ((zr * NX + x, rep), (zl * NX + x, rep)):
        pl.semaphore_signal(rdy.at[4], inc=1, device_id=dev, device_id_type=MESH)

    g_up = rcopy(gbuf.at[2, rows], gbuf.at[0, rows], hss.at[0], hrs.at[0], (d_up, rep))
    g_down = rcopy(
        gbuf.at[1, rows], gbuf.at[3, rows], hss.at[1], hrs.at[1], (lax.rem(d + NX * NZ - 1, NX * NZ), rep)
    )
    go(g_up, d < NX * NZ - 1)
    go(g_down, d > 0)
    expect("g_low", g_up, d > 0)
    expect("g_high", g_down, d < NX * NZ - 1)

    for key in (("g", 1), ("g", 3), ("g", 2)):
        got(key)
    lane = lax.rem(lax.broadcasted_iota(jnp.int32, (64, 512), 1), 16)
    for q in range(NX):
        t = gtall[q].astype(F32)
        cols = slice(q * 512, q * 512 + 512)
        g3[0:64, cols] = jnp.where(lane <= 14, pltpu.roll(t, 511, 1), 0.0).astype(BF16)
        g3[64:128, cols] = t.astype(BF16)
        g3[128:192, cols] = jnp.where(lane >= 1, pltpu.roll(t, 1, 1), 0.0).astype(BF16)


    for b in (3, 4, 5, 0, 1, 2, 6, 7, 8):
        if b == 0:
            got("low1")
            got("high1")
        kd, kh = b // 3, b % 3
        field = x10[kd : kd + 8, kh * 16 : kh * 16 + 256, :].reshape(2048, 256)
        out = jnp.dot(g3[...], field, preferred_element_type=F32)
        out = jnp.concatenate([out, out[128:192]], axis=0).T
        pair, twice = out[:, 0:128], out[:, 128:256]
        swapped = pltpu.roll(pair, 64, 1)
        for kw in range(3):
            start = (3 * b + kw) * 256
            at = start
            while at < start + 256:
                block = at // 216
                end = min(start + 256, (block + 1) * 216)
                k, q = block // 4, block % 4
                side, h = q // 2, q % 2
                source = twice if kw == 2 else (pair if kw == side else swapped)
                acc[k, h, at - block * 216 : end - block * 216, side * 64 : side * 64 + 64] = source[
                    at - start : end - start, side * 64 : side * 64 + 64
                ]
                at = end

    def ready(t):
        for dev in near:
            pl.semaphore_signal(rdy.at[t], inc=1, device_id=dev, device_id_type=MESH)

    half_of = (0, 1)

    def far(side, dist):
        return lax.rem(z + dist, NZ) if side == 0 else lax.rem(z + NZ - dist, NZ)

    hops = {"a": (4, 3), "b": (3, 2), "c": (2, 1), "d": (1, 1)}

    def unit(side, kind, h):
        dist, step = hops[kind]
        there = far(side, step) * NX + x
        if kind == "d":
            src, dst, n = acc.at[far(side, 1), h], rsb.at[side, h], 6 + h
        else:
            n = "abc".index(kind) * 2 + h
            src, dst = nsend.at[side, n], nrecv.at[side, n]
        return rcopy(src, dst, rss.at[side, n], rrs.at[side, n], (there, rep))

    def send_unit(side, kind, h):
        dist, _ = hops[kind]
        k = far(side, dist)
        if kind == "d":
            got(("rs", side, "b", h))
            got(("rs", side, "c", h))
            value = acc[k, h] + nrecv[side, 2 + h].astype(F32) + nrecv[side, 4 + h].astype(F32)
            if h == half_of[side]:
                got(("rs", side, "a", h))
                value = value + nrecv[side, h].astype(F32)
            acc[k, h] = value
        else:
            nsend[side, "abc".index(kind) * 2 + h] = acc[k, h].astype(BF16)
        go(unit(side, kind, h))
        expect(("rs", side, kind, h), unit(side, kind, h))

    pl.semaphore_wait(rdy.at[4], 2)
    ready(0)
    for h in (1, 0):
        send_unit(half_of.index(h), "a", h)
        for kind in ("b", "c"):
            for side in range(2):
                send_unit(side, kind, h)

    got("g_low")
    got("g_high")
    nt = (((1,), (1,)), ((), ()))

    def field_grad(p):
        lhs = jnp.concatenate(
            [
                gbuf[2 + p - kd, (2 - kh) * 16 : (2 - kh) * 16 + 256, :]
                for kd in range(3)
                for kh in range(3)
            ],
            axis=1,
        )
        y = []
        for kw in range(3):
            rhs = jnp.concatenate([wk[b, kw] for b in range(9)], axis=1)
            y.append(lax.dot_general(lhs, rhs, nt, preferred_element_type=F32))
        total = (
            y[1]
            + jnp.where(w_of <= 14, pltpu.roll(y[0], 255, 0), 0.0)
            + jnp.where(w_of >= 1, pltpu.roll(y[2], 1, 0), 0.0)
        )
        gout[p] = total.astype(BF16)

    pl.semaphore_wait(rdy.at[0], 3)
    ready(1)
    field_grad(0)
    for side in range(2):
        send_unit(side, "d", 1)
    for side in range(2):
        send_unit(side, "d", 0)
    pl.semaphore_wait(rdy.at[1], 3)
    ready(2)
    field_grad(1)
    pl.semaphore_wait(rdy.at[2], 3)

    which = lax.broadcasted_iota(jnp.int32, (56, 128), 1) // 32
    for h in range(2):
        rfin[h, 216:224, :] = jnp.zeros((8, 128), F32)

    def owner_copy(q, j):
        return rcopy(
            fsend.at[2 * q + j], frecv.at[rep], fss.at[2 * q + j], frs.at[rep], (z * NX + q, 2 * x + j)
        )

    def owner_local(q, j):
        return pltpu.make_async_copy(fsend.at[2 * q + j], frecv.at[rep], fss.at[2 * q + j])

    for h in (1, 0):
        total = acc[z, h]
        for side in range(2):
            got(("rs", side, "d", h))
            total = total + rsb[side, h]
        rfin[h, 0:216, :] = total * FACTOR
        for side in range(2):
            q = 2 * side + h
            for j in range(2):
                packed = jnp.zeros((56, 128), F32)
                for m in range(4):
                    part = rfin[h, m * 56 : m * 56 + 56, :]
                    shift = (32 * (m - 2 * side - j)) % 128
                    if shift:
                        part = pltpu.roll(part, shift, 1)
                    packed = jnp.where(which == m, part, packed)
                fsend[2 * q + j] = packed
                here = (x == q) & (rep == 2 * x + j)

                pl.when(here)(owner_local(q, j).start)
                go(owner_copy(q, j), jnp.logical_not(here))

    for v in range(NR):
        mine = (x == rep // 2) & (rep == v)
        copy = rcopy(fsend.at[v], frecv.at[v], fss.at[v], frs.at[v], (d, lax.rem(rep + 1, NR)))
        expect(("own", v), copy, jnp.logical_not(mine))
    for q in range(NX):
        for j in range(2):
            pl.when((x == q) & (rep == 2 * x + j))(owner_local(q, j).wait)
    for v in range(NR):
        got(("own", v))

    lanes = lax.broadcasted_iota(jnp.int32, (8, 128), 1)
    pairs = [(u, v) for u in range(NR) for v in range(u, NR)]
    part = jnp.zeros((8, 128), F32)
    for n, (u, v) in enumerate(pairs):
        prod = frecv[u] * frecv[v]
        total = prod[0:8]
        for m in range(1, 7):
            total = total + prod[8 * m : 8 * m + 8]
        part = jnp.where(lanes == n, jnp.sum(total, axis=1, keepdims=True), part)

    part = jnp.sum(part, axis=0, keepdims=True)

    gsrc[0] = part
    partner = rcopy(gsrc.at[0], gr1.at[0], a1s.at[0], a1r.at[0], near[0])
    go(partner)
    expect("partner", partner)
    got("partner")
    part = part + gr1[0]
    gsrc[1] = part
    chips = NX * NZ * NR // 2
    chip = d * (NR // 2) + rep // 2
    gr2[chip] = part

    def tell(i, _):
        other = lax.rem(chip + i, chips)
        dev = (other // (NR // 2), lax.rem(other, NR // 2) * 2 + core)
        rcopy(gsrc.at[1], gr2.at[chip], a2s.at[0], a2r.at[0], dev).start()
        return 0

    lax.fori_loop(1, chips, tell, 0)
    rest = gr2.at[pl.ds(0, chips - 1)]
    told = rcopy(rest, rest, a2s.at[0], a2r.at[0], near[0])
    told.wait_recv()
    told.wait_send()
    part = jnp.sum(gr2[...], axis=0)
    whole = part
    row = lanes[0:1]
    gram = {
        uv: jnp.sum(jnp.where(row == n, whole, 0.0), axis=1, keepdims=True)
        for n, uv in enumerate(pairs)
    }
    weights = adasum_weights(gram)
    merged = weights[0] * frecv[0]
    for v in range(1, NR):
        merged = merged + weights[v] * frecv[v]
    turned = merged.T
    for m in range(4):
        count = min(56, 216 - 56 * m)
        mout[:, m * 56 : m * 56 + count] = turned[m * 32 : m * 32 + 32, 0:count]

    finish()


def shards(volume, cotangent, kernel_weights):
    dma = pltpu.SemaphoreType.DMA
    any_space = pl.BlockSpec(memory_space=pl.ANY)
    vmem = pl.BlockSpec(memory_space=pltpu.VMEM)
    gout, mout = pl.pallas_call(
        kernel,
        name="adasum_step",
        out_shape=(
            pltpu.VMEM((2, 256, 256), BF16),
            pltpu.VMEM((32, 216), F32),
        ),
        in_specs=[any_space] * 3,
        out_specs=(vmem, vmem),
        scratch_shapes=[
            pltpu.VMEM((10, 288, 256), BF16),
            pltpu.VMEM((9, 3, 256, 256), BF16),
            pltpu.VMEM((2, 256, 256), BF16),
            pltpu.VMEM((2, 3, 256, 256), F32),
            pltpu.VMEM((4, 288, 256), BF16),
            pltpu.VMEM((4, 64, 512), BF16),
            pltpu.VMEM((4, 64, 512), BF16),
            pltpu.VMEM((192, 2048), BF16),
            pltpu.VMEM((8, 2, 216, 128), F32),
            pltpu.VMEM((2, 2, 216, 128), F32),
            pltpu.VMEM((2, 6, 216, 128), BF16),
            pltpu.VMEM((2, 6, 216, 128), BF16),
            pltpu.VMEM((2, 224, 128), F32),
            pltpu.VMEM((8, 56, 128), F32),
            pltpu.VMEM((8, 56, 128), F32),
            pltpu.VMEM((1, 1, 128), F32),
            pltpu.VMEM((128, 1, 128), F32),
            pltpu.VMEM((2, 1, 128), F32),
            dma((4,)),
            pltpu.SemaphoreType.REGULAR((5,)),
            dma((10,)), dma((8,)),
            dma((4,)), dma((4,)),
            dma((2,)), dma((2,)),
            dma((2, 8)), dma((2, 8)),
            dma((8,)), dma((8,)),
            dma((1,)), dma((1,)),
            dma((1,)), dma((1,)),
        ],
        compiler_params=pltpu.CompilerParams(
            collective_id=0, has_side_effects=True, vmem_limit_bytes=56 * 1024 * 1024
        ),
    )(
        volume.reshape(2, 256, 256),
        cotangent.reshape(2, 256, 256),
        kernel_weights.reshape(9, 3, 256, 256),
    )
    return gout.reshape(1, 2, 16, 16, 256), mout.T


def solution(mesh):
    return jax.shard_map(
        shards,
        mesh=mesh,
        in_specs=(P("replica", "depth"), P("replica", "depth"), P()),
        out_specs=(P("replica", "depth"), P("depth", "replica")),
        check_vma=False,
    )
```

```python
import functools

import jax
import jax.numpy as jnp
from jax import lax
from jax.experimental import pallas as pl
from jax.experimental.pallas import tpu as pltpu
from jax.sharding import PartitionSpec as P

MESH = pl.DeviceIdType.MESH
EPS = 1e-06
F32, BF16 = jnp.float32, jnp.bfloat16
NX, NZ, NR = 4, 8, 8
FACTOR = 1.0 / 128.0

def rcopy(src, dst, ss, rs, dev):
    return pltpu.make_async_remote_copy(
        src_ref=src, dst_ref=dst, send_sem=ss, recv_sem=rs, device_id=dev, device_id_type=MESH
    )


def adasum_weights(gram):
    dots = dict(gram)
    count = NR
    weights = [None] * NR
    members = [[v] for v in range(NR)]
    while count > 1:
        alpha = [None] * count
        for a in range(0, count, 2):
            b = a + 1
            half = 0.5 * dots[(a, b)]
            alpha[a] = 1.0 - half / (jnp.maximum(dots[(a, a)], 0.0) + EPS)
            alpha[b] = 1.0 - half / (jnp.maximum(dots[(b, b)], 0.0) + EPS)
        for a in range(count):
            for v in members[a]:
                weights[v] = alpha[a] if weights[v] is None else weights[v] * alpha[a]
        merged = {}
        half_count = count // 2
        for i in range(half_count):
            for j in range(i, half_count):
                total = None
                for a in (2 * i, 2 * i + 1):
                    for b in (2 * j, 2 * j + 1):
                        term = alpha[a] * alpha[b] * dots[(min(a, b), max(a, b))]
                        total = term if total is None else total + term
                merged[(i, j)] = total
        members = [members[2 * i] + members[2 * i + 1] for i in range(half_count)]
        dots = merged
        count = half_count
    return weights


def kernel(
    vol, cot, kern,
    gout, mout,
    x10, wk, cotv, ybuf, gbuf, gts, gtall, g3, acc, rsb, nsend, nrecv, rfin, fsend, frecv, gr1, gr2, gsrc,
    lsem, rdy, xss, xrs, gss, grs, hss, hrs, rss, rrs, fss, frs, a1s, a1r, a2s, a2r,
):
    d = lax.axis_index("depth")
    rep = lax.axis_index("replica")
    z = d // NX
    x = lax.rem(d, NX)
    xr, xl = lax.rem(x + 1, NX), lax.rem(x + 3, NX)
    xo = lax.rem(x + 2, NX)
    zr, zl = lax.rem(z + 1, NZ), lax.rem(z + 7, NZ)

    sends, expected = [], {}

    def go(copy, cond=None):
        sends.append((copy, cond))
        if cond is None:
            copy.start()
        else:
            pl.when(cond)(copy.start)

    def expect(key, copy, cond=None):
        expected[key] = (copy, cond)

    def got(key):
        copy, cond = expected.pop(key)
        if cond is None:
            copy.wait_recv()
        else:
            pl.when(cond)(copy.wait_recv)

    def finish():
        for key in list(expected):
            got(key)
        for copy, cond in sends:
            if cond is None:
                copy.wait_send()
            else:
                pl.when(cond)(copy.wait_send)

    bar = pltpu.get_barrier_semaphore()

    def greet(dd, rr):
        pl.semaphore_signal(bar, inc=1, device_id=(dd, rr), device_id_type=MESH)

    core = lax.rem(rep, 2)
    near = [
        (d, rep + 1 - 2 * core),
        (d, lax.rem(rep + 2, NR)),
        (d, lax.rem(rep + 6, NR)),
    ]
    for dev in near + [(z * NX + xo, rep), (z * NX + xr, rep), (z * NX + xl, rep), (zr * NX + x, rep), (zl * NX + x, rep)]:
        greet(*dev)

    d_up, d_down = lax.rem(d + 1, NX * NZ), lax.rem(d + NX * NZ - 1, NX * NZ)
    at_top, at_bottom = (x == 3) & (z < NZ - 1), (x == 0) & (z > 0)
    pl.when(at_top)(lambda: greet(d_up, rep))
    pl.when(at_bottom)(lambda: greet(d_down, rep))

    rows = pl.ds(16, 256)
    lx = [pltpu.make_async_copy(vol.at[p], x10.at[1 + 2 * x + p, rows], lsem.at[p]) for p in range(2)]
    lw = pltpu.make_async_copy(kern, wk, lsem.at[2])
    lc = pltpu.make_async_copy(cot, cotv, lsem.at[3])
    for c in lx:
        c.start()
    lw.start()
    lc.start()
    pad = jnp.zeros((16, 256), BF16)
    for k in range(10):
        x10[k, 0:16, :] = pad
        x10[k, 272:288, :] = pad
    for k in range(4):
        gbuf[k, 0:16, :] = pad
        gbuf[k, 272:288, :] = pad

    @pl.when(z == 0)
    def _():
        x10[0, 16:272, :] = jnp.zeros((256, 256), BF16)

    @pl.when(z == NZ - 1)
    def _():
        x10[9, 16:272, :] = jnp.zeros((256, 256), BF16)

    @pl.when(d == 0)
    def _():
        gbuf[0, 16:272, :] = jnp.zeros((256, 256), BF16)

    @pl.when(d == NX * NZ - 1)
    def _():
        gbuf[3, 16:272, :] = jnp.zeros((256, 256), BF16)

    pl.semaphore_wait(bar, 8 + (at_top | at_bottom).astype(jnp.int32))

    dr_, dl_ = z * NX + xr, z * NX + xl

    def plane(owner, p):
        return x10.at[1 + 2 * owner + p, rows]

    def to_right(p):
        return rcopy(vol.at[p], plane(x, p), xss.at[p], xrs.at[p], (dr_, rep))

    def to_left(p):
        return rcopy(vol.at[p], plane(x, p), xss.at[2 + p], xrs.at[2 + p], (dl_, rep))

    def from_left(p):
        return rcopy(vol.at[p], plane(xl, p), xss.at[p], xrs.at[p], (dr_, rep))

    def from_right(p):
        return rcopy(vol.at[p], plane(xr, p), xss.at[2 + p], xrs.at[2 + p], (dl_, rep))

    relay_r = rcopy(plane(xl, 1), plane(xl, 1), xss.at[4], xrs.at[4], (dr_, rep))
    relay_l = rcopy(plane(xr, 0), plane(xr, 0), xss.at[5], xrs.at[5], (dl_, rep))
    from_relay_l = rcopy(plane(xo, 1), plane(xo, 1), xss.at[4], xrs.at[4], (dr_, rep))
    from_relay_r = rcopy(plane(xo, 0), plane(xo, 0), xss.at[5], xrs.at[5], (dl_, rep))

    low, high = x10.at[0, rows], x10.at[9, rows]
    up_first = rcopy(vol.at[1], low, xss.at[6], xrs.at[6], (d_up, rep))
    down_first = rcopy(vol.at[0], high, xss.at[7], xrs.at[7], (d_down, rep))
    up = rcopy(x10.at[8, rows], low, xss.at[8], xrs.at[6], (zr * NX + x, rep))
    down = rcopy(x10.at[1, rows], high, xss.at[9], xrs.at[7], (zl * NX + x, rep))
    is_low, is_high = z > 0, z < NZ - 1

    go(up_first, at_top)
    go(down_first, at_bottom)
    go(to_right(1))
    go(to_left(0))
    go(to_right(0))
    go(to_left(1))
    for dev in ((zr * NX + x, rep), (zl * NX + x, rep)):
        pl.semaphore_signal(rdy.at[3], inc=1, device_id=dev, device_id_type=MESH)
    for c in lx:
        c.wait()
    go(up, is_high & (x == 3))
    go(down, is_low & (x == 0))
    for p in range(2):
        expect(("left", p), from_left(p))
        expect(("right", p), from_right(p))
    expect("low0", up, at_bottom)
    expect("high0", down, at_top)
    expect("low1", up, is_low & (x != 0))
    expect("high1", down, is_high & (x != 3))
    expect("relay_l", from_relay_l)
    expect("relay_r", from_relay_r)

    lw.wait()
    for p in range(2):
        taps = [(kd, kh) for kd in ((1, 2) if p == 0 else (0, 1)) for kh in range(3)]
        lhs = jnp.concatenate(
            [x10[2 * x + p + kd, kh * 16 : kh * 16 + 256, :] for kd, kh in taps], axis=1
        )
        for kw in range(3):
            rhs = jnp.concatenate([wk[kd * 3 + kh, kw] for kd, kh in taps], axis=0)
            ybuf[p, kw] = jnp.dot(lhs, rhs, preferred_element_type=F32)
    lc.wait()

    got(("left", 1))
    go(relay_r)
    got(("right", 0))
    go(relay_l)
    got("low0")
    got("high0")
    w_of = lax.rem(lax.broadcasted_iota(jnp.int32, (256, 256), 0), 16)
    for p in range(2):
        kd = 0 if p == 0 else 2
        lhs = jnp.concatenate(
            [x10[2 * x + p + kd, kh * 16 : kh * 16 + 256, :] for kh in range(3)], axis=1
        )
        y = []
        for kw in range(3):
            rhs = jnp.concatenate([wk[kd * 3 + kh, kw] for kh in range(3)], axis=0)
            y.append(ybuf[p, kw] + jnp.dot(lhs, rhs, preferred_element_type=F32))
        preact = (
            y[1]
            + jnp.where(w_of >= 1, pltpu.roll(y[0], 1, 0), 0.0)
            + jnp.where(w_of <= 14, pltpu.roll(y[2], 255, 0), 0.0)
        )
        s = jax.nn.sigmoid(preact)
        g = (cotv[p].astype(F32) * s * (1.0 + preact * (1.0 - s))).astype(BF16)
        gbuf[1 + p, 16:272, :] = g
        gt = g.astype(F32).T.astype(BF16)
        for q in range(NX):
            gts[q, :, p * 256 : p * 256 + 256] = gt[q * 64 : q * 64 + 64, :]

    def g_send(dx):
        q = lax.rem(x + dx, NX)
        return rcopy(gts.at[q], gtall.at[x], gss.at[dx], grs.at[dx], (z * NX + q, rep))

    def g_recv(dx):
        q = lax.rem(x + NX - dx, NX)
        return rcopy(gts.at[q], gtall.at[q], gss.at[dx], grs.at[dx], (z * NX + q, rep))

    for dx in (1, 3, 2):
        go(g_send(dx))
        expect(("g", dx), g_recv(dx))
    gtall[x] = gts[x]

    got(("left", 0))
    got(("right", 1))
    got("relay_l")
    got("relay_r")
    inner = (x == 1) | (x == 2)
    go(up, is_high & inner)
    go(down, is_low & inner)
    pl.semaphore_wait(rdy.at[3], 2)
    for dev in ((zr * NX + x, rep), (zl * NX + x, rep)):
        pl.semaphore_signal(rdy.at[4], inc=1, device_id=dev, device_id_type=MESH)

    g_up = rcopy(gbuf.at[2, rows], gbuf.at[0, rows], hss.at[0], hrs.at[0], (d_up, rep))
    g_down = rcopy(
        gbuf.at[1, rows], gbuf.at[3, rows], hss.at[1], hrs.at[1], (lax.rem(d + NX * NZ - 1, NX * NZ), rep)
    )
    go(g_up, d < NX * NZ - 1)
    go(g_down, d > 0)
    expect("g_low", g_up, d > 0)
    expect("g_high", g_down, d < NX * NZ - 1)

    for key in (("g", 1), ("g", 3), ("g", 2)):
        got(key)
    lane = lax.rem(lax.broadcasted_iota(jnp.int32, (64, 512), 1), 16)
    for q in range(NX):
        t = gtall[q].astype(F32)
        cols = slice(q * 512, q * 512 + 512)
        g3[0:64, cols] = jnp.where(lane <= 14, pltpu.roll(t, 511, 1), 0.0).astype(BF16)
        g3[64:128, cols] = t.astype(BF16)
        g3[128:192, cols] = jnp.where(lane >= 1, pltpu.roll(t, 1, 1), 0.0).astype(BF16)


    for b in (3, 4, 5, 0, 1, 2, 6, 7, 8):
        if b == 0:
            got("low1")
            got("high1")
        kd, kh = b // 3, b % 3
        field = x10[kd : kd + 8, kh * 16 : kh * 16 + 256, :].reshape(2048, 256)
        out = jnp.dot(g3[...], field, preferred_element_type=F32)
        out = jnp.concatenate([out, out[128:192]], axis=0).T
        pair, twice = out[:, 0:128], out[:, 128:256]
        swapped = pltpu.roll(pair, 64, 1)
        for kw in range(3):
            start = (3 * b + kw) * 256
            at = start
            while at < start + 256:
                block = at // 216
                end = min(start + 256, (block + 1) * 216)
                k, q = block // 4, block % 4
                side, h = q // 2, q % 2
                source = twice if kw == 2 else (pair if kw == side else swapped)
                acc[k, h, at - block * 216 : end - block * 216, side * 64 : side * 64 + 64] = source[
                    at - start : end - start, side * 64 : side * 64 + 64
                ]
                at = end

    def ready(t):
        for dev in near:
            pl.semaphore_signal(rdy.at[t], inc=1, device_id=dev, device_id_type=MESH)

    half_of = (0, 1)

    def far(side, dist):
        return lax.rem(z + dist, NZ) if side == 0 else lax.rem(z + NZ - dist, NZ)

    hops = {"a": (4, 3), "b": (3, 2), "c": (2, 1), "d": (1, 1)}

    def unit(side, kind, h):
        dist, step = hops[kind]
        there = far(side, step) * NX + x
        if kind == "d":
            src, dst, n = acc.at[far(side, 1), h], rsb.at[side, h], 6 + h
        else:
            n = "abc".index(kind) * 2 + h
            src, dst = nsend.at[side, n], nrecv.at[side, n]
        return rcopy(src, dst, rss.at[side, n], rrs.at[side, n], (there, rep))

    def send_unit(side, kind, h):
        dist, _ = hops[kind]
        k = far(side, dist)
        if kind == "d":
            got(("rs", side, "b", h))
            got(("rs", side, "c", h))
            value = acc[k, h] + nrecv[side, 2 + h].astype(F32) + nrecv[side, 4 + h].astype(F32)
            if h == half_of[side]:
                got(("rs", side, "a", h))
                value = value + nrecv[side, h].astype(F32)
            acc[k, h] = value
        else:
            nsend[side, "abc".index(kind) * 2 + h] = acc[k, h].astype(BF16)
        go(unit(side, kind, h))
        expect(("rs", side, kind, h), unit(side, kind, h))

    pl.semaphore_wait(rdy.at[4], 2)
    ready(0)
    for h in (1, 0):
        send_unit(half_of.index(h), "a", h)
        for kind in ("b", "c"):
            for side in range(2):
                send_unit(side, kind, h)

    got("g_low")
    got("g_high")
    nt = (((1,), (1,)), ((), ()))

    def field_grad(p):
        lhs = jnp.concatenate(
            [
                gbuf[2 + p - kd, (2 - kh) * 16 : (2 - kh) * 16 + 256, :]
                for kd in range(3)
                for kh in range(3)
            ],
            axis=1,
        )
        y = []
        for kw in range(3):
            rhs = jnp.concatenate([wk[b, kw] for b in range(9)], axis=1)
            y.append(lax.dot_general(lhs, rhs, nt, preferred_element_type=F32))
        total = (
            y[1]
            + jnp.where(w_of <= 14, pltpu.roll(y[0], 255, 0), 0.0)
            + jnp.where(w_of >= 1, pltpu.roll(y[2], 1, 0), 0.0)
        )
        gout[p] = total.astype(BF16)

    pl.semaphore_wait(rdy.at[0], 3)
    ready(1)
    field_grad(0)
    for side in range(2):
        send_unit(side, "d", 1)
    for side in range(2):
        send_unit(side, "d", 0)
    pl.semaphore_wait(rdy.at[1], 3)
    ready(2)
    field_grad(1)
    pl.semaphore_wait(rdy.at[2], 3)

    which = lax.broadcasted_iota(jnp.int32, (56, 128), 1) // 32
    for h in range(2):
        rfin[h, 216:224, :] = jnp.zeros((8, 128), F32)

    def owner_copy(q, j):
        return rcopy(
            fsend.at[2 * q + j], frecv.at[rep], fss.at[2 * q + j], frs.at[rep], (z * NX + q, 2 * x + j)
        )

    def owner_local(q, j):
        return pltpu.make_async_copy(fsend.at[2 * q + j], frecv.at[rep], fss.at[2 * q + j])

    for h in (1, 0):
        total = acc[z, h]
        for side in range(2):
            got(("rs", side, "d", h))
            total = total + rsb[side, h]
        rfin[h, 0:216, :] = total * FACTOR
        for side in range(2):
            q = 2 * side + h
            for j in range(2):
                packed = jnp.zeros((56, 128), F32)
                for m in range(4):
                    part = rfin[h, m * 56 : m * 56 + 56, :]
                    shift = (32 * (m - 2 * side - j)) % 128
                    if shift:
                        part = pltpu.roll(part, shift, 1)
                    packed = jnp.where(which == m, part, packed)
                fsend[2 * q + j] = packed
                here = (x == q) & (rep == 2 * x + j)

                pl.when(here)(owner_local(q, j).start)
                go(owner_copy(q, j), jnp.logical_not(here))

    for v in range(NR):
        mine = (x == rep // 2) & (rep == v)
        copy = rcopy(fsend.at[v], frecv.at[v], fss.at[v], frs.at[v], (d, lax.rem(rep + 1, NR)))
        expect(("own", v), copy, jnp.logical_not(mine))
    for q in range(NX):
        for j in range(2):
            pl.when((x == q) & (rep == 2 * x + j))(owner_local(q, j).wait)
    for v in range(NR):
        got(("own", v))

    lanes = lax.broadcasted_iota(jnp.int32, (8, 128), 1)
    pairs = [(u, v) for u in range(NR) for v in range(u, NR)]
    part = jnp.zeros((8, 128), F32)
    for n, (u, v) in enumerate(pairs):
        prod = frecv[u] * frecv[v]
        total = prod[0:8]
        for m in range(1, 7):
            total = total + prod[8 * m : 8 * m + 8]
        part = jnp.where(lanes == n, jnp.sum(total, axis=1, keepdims=True), part)

    part = jnp.sum(part, axis=0, keepdims=True)

    gsrc[0] = part
    partner = rcopy(gsrc.at[0], gr1.at[0], a1s.at[0], a1r.at[0], near[0])
    go(partner)
    expect("partner", partner)
    got("partner")
    part = part + gr1[0]
    gsrc[1] = part
    chips = NX * NZ * NR // 2
    chip = d * (NR // 2) + rep // 2
    gr2[chip] = part

    def tell(i, _):
        other = lax.rem(chip + i, chips)
        dev = (other // (NR // 2), lax.rem(other, NR // 2) * 2 + core)
        rcopy(gsrc.at[1], gr2.at[chip], a2s.at[0], a2r.at[0], dev).start()
        return 0

    lax.fori_loop(1, chips, tell, 0)
    rest = gr2.at[pl.ds(0, chips - 1)]
    told = rcopy(rest, rest, a2s.at[0], a2r.at[0], near[0])
    told.wait_recv()
    told.wait_send()
    part = jnp.sum(gr2[...], axis=0)
    whole = part
    row = lanes[0:1]
    gram = {
        uv: jnp.sum(jnp.where(row == n, whole, 0.0), axis=1, keepdims=True)
        for n, uv in enumerate(pairs)
    }
    weights = adasum_weights(gram)
    merged = weights[0] * frecv[0]
    for v in range(1, NR):
        merged = merged + weights[v] * frecv[v]
    turned = merged.T
    for m in range(4):
        count = min(56, 216 - 56 * m)
        mout[:, m * 56 : m * 56 + count] = turned[m * 32 : m * 32 + 32, 0:count]

    finish()


def shards(volume, cotangent, kernel_weights):
    dma = pltpu.SemaphoreType.DMA
    any_space = pl.BlockSpec(memory_space=pl.ANY)
    vmem = pl.BlockSpec(memory_space=pltpu.VMEM)
    gout, mout = pl.pallas_call(
        kernel,
        name="adasum_step",
        out_shape=(
            pltpu.VMEM((2, 256, 256), BF16),
            pltpu.VMEM((32, 216), F32),
        ),
        in_specs=[any_space] * 3,
        out_specs=(vmem, vmem),
        scratch_shapes=[
            pltpu.VMEM((10, 288, 256), BF16),
            pltpu.VMEM((9, 3, 256, 256), BF16),
            pltpu.VMEM((2, 256, 256), BF16),
            pltpu.VMEM((2, 3, 256, 256), F32),
            pltpu.VMEM((4, 288, 256), BF16),
            pltpu.VMEM((4, 64, 512), BF16),
            pltpu.VMEM((4, 64, 512), BF16),
            pltpu.VMEM((192, 2048), BF16),
            pltpu.VMEM((8, 2, 216, 128), F32),
            pltpu.VMEM((2, 2, 216, 128), F32),
            pltpu.VMEM((2, 6, 216, 128), BF16),
            pltpu.VMEM((2, 6, 216, 128), BF16),
            pltpu.VMEM((2, 224, 128), F32),
            pltpu.VMEM((8, 56, 128), F32),
            pltpu.VMEM((8, 56, 128), F32),
            pltpu.VMEM((1, 1, 128), F32),
            pltpu.VMEM((128, 1, 128), F32),
            pltpu.VMEM((2, 1, 128), F32),
            dma((4,)),
            pltpu.SemaphoreType.REGULAR((5,)),
            dma((10,)), dma((8,)),
            dma((4,)), dma((4,)),
            dma((2,)), dma((2,)),
            dma((2, 8)), dma((2, 8)),
            dma((8,)), dma((8,)),
            dma((1,)), dma((1,)),
            dma((1,)), dma((1,)),
        ],
        compiler_params=pltpu.CompilerParams(
            collective_id=0, has_side_effects=True, vmem_limit_bytes=56 * 1024 * 1024
        ),
    )(
        volume.reshape(2, 256, 256),
        cotangent.reshape(2, 256, 256),
        kernel_weights.reshape(9, 3, 256, 256),
    )
    return gout.reshape(1, 2, 16, 16, 256), mout.T


def solution(mesh):
    return jax.shard_map(
        shards,
        mesh=mesh,
        in_specs=(P("replica", "depth"), P("replica", "depth"), P()),
        out_specs=(P("replica", "depth"), P("depth", "replica")),
        check_vma=False,
    )
```
